128 devices in a mesh: grp: 16 (over x, y), mem: 8 (over z, core).
Axes of the slice: x: 4, y: 4, z: 4, core: 2. Of those that a mesh axis runs over, the one named last changes fastest.
Arguments:
- filterbank: float32 [16, 8, 8, 16000], P('grp', 'mem'), may hold values from -6 to 6
- destination: int32 [16, 64], P('grp', 'mem'), may hold values from 0 to 15, as said below
- initial_conv_weight: bfloat16 [400, 1024], replicated, may hold values from -0.3125 to 0.3125
- expand_weight: bfloat16 [1024, 1024], replicated, may hold values from -0.1875 to 0.1875
- branch_weight: bfloat16 [7, 384, 128], replicated, may hold values from -0.3125 to 0.3125
- merge_weight: bfloat16 [1024, 1024], replicated, may hold values from -0.1875 to 0.1875
- squeeze_weight: bfloat16 [1024, 128], replicated, may hold values from -0.1875 to 0.1875
- excite_weight: bfloat16 [128, 1024], replicated, may hold values from -0.5 to 0.5
- attend_weight: bfloat16 [16, 3072, 128], P('grp'), may hold values from -0.1875 to 0.1875
- score_weight: bfloat16 [16, 128, 1024], P('grp'), may hold values from -0.5 to 0.5
- embed_weight: bfloat16 [16, 2048, 192], P('grp'), may hold values from -0.125 to 0.125
- language_weight: bfloat16 [16, 192, 107], P('grp'), may hold values from -0.4375 to 0.4375
Outputs:
- language_logits: float32 [16, 64, 107], P('grp', 'mem')
- similarity: float32 [16, 64, 64], P('grp', 'mem')
The draws below stay inside these ranges and needn't reach their ends.
Inputs may be any that keep to these rules, and one draw needn't show every extreme that they name: `destination`: each device sends its 8 segments to 8 different groups, so at most 1 to any group. For every index of mem, one group receives exactly 16 segments from the devices of that index, and no group receives more.
All inputs are finite; a program needn't handle non-finite values.
Results may differ from the reference program's by a relative error of at most 0.0075.
Values may be sent and summed in bfloat16 or wider, within the bound.
No kernel may reach another device: no remote copies, remote signals or barrier semaphores. Data moves between devices by JAX's collectives and lax.ppermute only.
A program may use at most 128 MiB of HBM per device.

```python
import jax
import jax.numpy as jnp
from jax import lax

MELS = 80
CH = 1024
SCALE = 8
BR = 128
KERN0 = 5
BRANCH_DILATION = 2
SE_DIM = 128
ATT = 128
EMB = 192
LANGS = 107
FRAMES = 200
STORE = 8
N_GRP = 16
N_MEM = 8


def permute_row(row_key, row_values):
    return jax.random.permutation(row_key, row_values)


def draw_destination(key, part):
    groups = N_GRP
    extra = min(STORE, groups - STORE)

    def one_member(member):
        member_key = jax.random.fold_in(key, member)
        ranking = jax.random.permutation(jax.random.fold_in(member_key, 1), groups)
        source = jnp.arange(groups, dtype=jnp.int32)[:, None]
        column = jnp.arange(STORE, dtype=jnp.int32)[None, :]
        picked = (source + column) % groups
        special = (column == STORE - 1) & (source >= 1) & (source <= extra)
        picked = jnp.where(special, 0, picked)
        placed = ranking[picked]
        row_keys = jax.random.split(jax.random.fold_in(member_key, 2), groups)
        placed = jax.vmap(permute_row)(row_keys, placed)
        relabel = jax.random.permutation(jax.random.fold_in(member_key, 3), groups)
        return placed[relabel]
    tables = jax.vmap(one_member)(jnp.arange(N_MEM, dtype=jnp.int32))
    return jnp.transpose(tables, (1, 0, 2)).reshape(groups, N_MEM * STORE).astype(jnp.int32)


def steps_of(key, extent, cuts, least, largest):
    gain = 1.0
    for position, parts in cuts:
        draws = jax.random.uniform(jax.random.fold_in(jax.random.fold_in(key, 6), position), (parts,), jnp.float32, least / len(cuts), largest / len(cuts))
        gain = gain * jnp.repeat(jnp.exp(draws), extent[position] // parts).reshape((-1,) + (1,) * (len(extent) - 1 - position))
    return gain


def noise(key, shape, deviation, limit, shards=(), kind=jnp.bfloat16):
    array = deviation * jax.random.normal(key, shape, jnp.float32)
    if shards:
        array = array * steps_of(key, shape, shards, -0.22, 0.18)
    return jnp.clip(array, -limit, limit).astype(kind)


def setup_inputs(seed: int = 0) -> dict:
    splits = jax.random.split(jax.random.key(seed), 13)
    return {
        "filterbank": noise(splits[0], (N_GRP, N_MEM, STORE, FRAMES * MELS), 1.0, 6.0, ((0, 16), (1, 8)), jnp.float32),
        "destination": draw_destination(jax.random.fold_in(splits[12], 71), 0),
        "initial_conv_weight": noise(splits[2], (KERN0 * MELS, CH), (KERN0 * MELS) ** -0.5, 0.3125),
        "expand_weight": noise(splits[3], (CH, CH), CH ** -0.5, 0.1875),
        "branch_weight": noise(splits[4], (SCALE - 1, 3 * BR, BR), (3 * BR) ** -0.5, 0.3125),
        "merge_weight": noise(splits[5], (CH, CH), CH ** -0.5, 0.1875),
        "squeeze_weight": noise(splits[6], (CH, SE_DIM), CH ** -0.5, 0.1875),
        "excite_weight": noise(splits[7], (SE_DIM, CH), SE_DIM ** -0.5, 0.5),
        "attend_weight": noise(splits[8], (N_GRP, 3 * CH, ATT), CH ** -0.5, 0.1875, ((0, 16),)),
        "score_weight": noise(splits[9], (N_GRP, ATT, CH), ATT ** -0.5, 0.5, ((0, 16),)),
        "embed_weight": noise(splits[10], (N_GRP, 2 * CH, EMB), (2 * CH) ** -0.5, 0.125, ((0, 16),)),
        "language_weight": noise(splits[11], (N_GRP, EMB, LANGS), EMB ** -0.5, 0.4375, ((0, 16),)),
    }


EPS_STAT = 1e-05
EPS_NORM = 1e-06

def offset_frames(values, radius, spacing):
    frames = values.shape[1]
    padded = jnp.pad(values, ((0, 0), (radius * spacing, radius * spacing), (0, 0)))
    return jnp.concatenate([padded[:, offset * spacing:offset * spacing + frames] for offset in range(2 * radius + 1)], axis=2)

def trunk(features, initial_conv_weight, expand_weight, branch_weight, merge_weight, squeeze_weight, excite_weight):
    lowered = features.astype(jnp.bfloat16)
    columns = offset_frames(lowered, 2, 1)
    front_out = jax.nn.relu(jnp.einsum('nfk,kc->nfc', columns, initial_conv_weight, preferred_element_type=jnp.float32)).astype(jnp.bfloat16)
    expanded = jax.nn.relu(jnp.einsum('nfk,kc->nfc', front_out, expand_weight, preferred_element_type=jnp.float32)).astype(jnp.bfloat16)
    branch_width = expanded.shape[2] // SCALE
    pieces = [expanded[:, :, :branch_width]]
    previous = expanded[:, :, :branch_width]
    for branch in range(1, SCALE):
        present_frames = expanded[:, :, branch * branch_width:(branch + 1) * branch_width]
        if branch > 1:
            present_frames = (present_frames.astype(jnp.float32) + previous.astype(jnp.float32)).astype(jnp.bfloat16)
        stacked_rows = offset_frames(present_frames, 1, BRANCH_DILATION)
        previous = jax.nn.relu(jnp.einsum('nfk,kc->nfc', stacked_rows, branch_weight[branch - 1], preferred_element_type=jnp.float32)).astype(jnp.bfloat16)
        pieces.append(previous)
    joined = jnp.concatenate(pieces, axis=2)
    merged = jax.nn.relu(jnp.einsum('nfk,kc->nfc', joined, merge_weight, preferred_element_type=jnp.float32))
    squeezed = lax.optimization_barrier(jnp.mean(merged, axis=1))
    hidden = jax.nn.relu(jnp.dot(squeezed, squeeze_weight.astype(jnp.float32), precision=lax.Precision.HIGHEST))
    excited = jax.nn.sigmoid(jnp.dot(hidden, excite_weight.astype(jnp.float32), precision=lax.Precision.HIGHEST))
    return (front_out.astype(jnp.float32) + merged * excited[:, None, :]).astype(jnp.bfloat16)

def head(trunk_out, attend_weight, score_weight, embed_weight, language_weight):
    channels = trunk_out.shape[1]
    widened = trunk_out.astype(jnp.float32)
    center = lax.optimization_barrier(jnp.mean(widened, axis=0))
    spread = jnp.sqrt(lax.optimization_barrier(jnp.mean(jnp.square(widened - center), axis=0)) + EPS_STAT)
    context = jnp.dot(center, attend_weight[channels:2 * channels].astype(jnp.float32), precision=lax.Precision.HIGHEST)
    context = context + jnp.dot(spread, attend_weight[2 * channels:].astype(jnp.float32), precision=lax.Precision.HIGHEST)
    attended = jnp.tanh(jnp.dot(trunk_out, attend_weight[:channels], preferred_element_type=jnp.float32) + context).astype(jnp.bfloat16)
    signal_energy = jnp.dot(attended, score_weight, preferred_element_type=jnp.float32)
    weights = jnp.exp(signal_energy)
    weights = weights / lax.optimization_barrier(jnp.sum(weights, axis=0))
    pooled_mean = lax.optimization_barrier(jnp.sum(weights * widened, axis=0))
    pooled_std = jnp.sqrt(lax.optimization_barrier(jnp.sum(weights * jnp.square(widened - pooled_mean), axis=0)) + EPS_STAT)
    pooled_features = jnp.concatenate([pooled_mean, pooled_std]).astype(jnp.bfloat16)
    embedding = jnp.dot(pooled_features, embed_weight, preferred_element_type=jnp.float32)
    logits = jnp.dot(embedding.astype(jnp.bfloat16), language_weight, preferred_element_type=jnp.float32)
    return (embedding, logits)

def reference(filterbank, destination, initial_conv_weight, expand_weight, branch_weight, merge_weight, squeeze_weight, excite_weight, attend_weight, score_weight, embed_weight, language_weight):
    segments = filterbank.reshape(-1, FRAMES, MELS)
    targets = destination.reshape(-1).astype(jnp.int32)

    def score_one(segment):
        features, target = segment
        trunk_out = trunk(features[None], initial_conv_weight, expand_weight, branch_weight, merge_weight, squeeze_weight, excite_weight)[0]
        return head(trunk_out, attend_weight[target], score_weight[target], embed_weight[target], language_weight[target])
    embedding, logits = lax.map(score_one, (segments, targets))
    normed = (embedding * lax.rsqrt(lax.optimization_barrier(jnp.mean(jnp.square(embedding), axis=1, keepdims=True)) + EPS_NORM)).astype(jnp.bfloat16)
    normed = normed.reshape(N_GRP, N_MEM * STORE, EMB).astype(jnp.float32)
    similarity = jnp.einsum('gie,gje->gij', normed, normed, precision=lax.Precision.HIGHEST) / EMB
    return (logits.reshape(N_GRP, N_MEM * STORE, LANGS), similarity)
```

```python
import functools

import jax
import jax.numpy as jnp
from jax import lax
from jax.experimental import pallas as pl
from jax.experimental.pallas import tpu as pltpu
from jax.sharding import PartitionSpec as P

MELS = 80
CH = 1024
BR = 128
SCALE = 8
ATT = 128
EMB = 192
LANGS = 107
FRAMES = 200
STORE = 8
SLOTS = 16
LANES = 128

FLAT = FRAMES * MELS // LANES
ROWS = 128

SUPER = 8
NSUPER = FRAMES // SUPER
WIDE = SUPER * MELS
BLOCKS = WIDE // LANES
TAPS = 5 * MELS
PAD_TOP = 112

EPS_STAT = 1e-05
EPS_NORM = 1e-06

F32 = jnp.float32
BF16 = jnp.bfloat16


def dot(a, b):
    return jnp.dot(a, b, preferred_element_type=F32)


def exact_dot(a, b):
    rows = a.shape[0]
    high = a.astype(BF16)
    rest = a - high.astype(F32)
    mid = rest.astype(BF16)
    low = (rest - mid.astype(F32)).astype(BF16)
    out = dot(jnp.concatenate([high, mid, low], axis=0), b)
    return out[:rows] + (out[rows : 2 * rows] + out[2 * rows :])


def pack_kernel(dest_ref, bank_ref, out_ref, row_ref):
    out_ref[...] = jnp.zeros_like(out_ref)
    for s in range(STORE):
        row_ref[:FLAT] = bank_ref[:, s, :]
        row_ref[FLAT:] = jnp.full((ROWS - FLAT, LANES), s + 1, F32)
        out_ref[dest_ref[s]] = row_ref[...].astype(BF16)


def pack(bank, dest):
    return pl.pallas_call(
        pack_kernel,
        out_shape=jax.ShapeDtypeStruct((SLOTS, ROWS, LANES), BF16),
        in_specs=[
            pl.BlockSpec(memory_space=pltpu.SMEM),
            pl.BlockSpec(memory_space=pltpu.VMEM),
        ],
        out_specs=pl.BlockSpec(memory_space=pltpu.VMEM),
        scratch_shapes=[pltpu.VMEM((ROWS, LANES), F32)],
        name="pack",
    )(dest, bank)


def family_kernel(
    recv_ref,
    front_w,
    expand_w,
    pair_w,
    merge_w,
    squeeze_w,
    excite_w,
    attend_w,
    score_w,
    embed_w,
    lang_w,
    out_ref,
    flat,
    bank,
    front,
    wide,
    joined,
    merged,
    pre,
    attended,
    total,
    first,
    second,
    third,
):
    mb = 20
    for s in range(SLOTS):
        flat[:, s, :] = recv_ref[s].astype(F32)
    header = flat[FLAT]
    bank[0] = jnp.zeros((SLOTS, WIDE), BF16)
    bank[NSUPER + 1] = jnp.zeros((SLOTS, WIDE), BF16)
    for r in range(NSUPER):
        bank[r + 1] = jnp.concatenate(
            [flat[BLOCKS * r + t].astype(BF16) for t in range(BLOCKS)], axis=1
        )

    def front_cols(n, carry):
        cols = pl.ds(pl.multiple_of(n * 256, 256), 256)
        for j in range(SUPER):
            start = MELS * (j - 2)
            block, offset = start // LANES, start % LANES
            pieces = []
            for t in range(block, block + 4):
                shift, lane = t // BLOCKS, t % BLOCKS
                pieces.append(
                    bank[1 + shift : 1 + shift + NSUPER, :, lane * LANES : (lane + 1) * LANES]
                )
            window = jnp.concatenate(pieces, axis=2).reshape(NSUPER * SLOTS, 4 * LANES)
            top = PAD_TOP - offset
            out = dot(window, front_w[top : top + 4 * LANES, cols])
            front[:, j, :, cols] = (
                jnp.maximum(out, 0.0).astype(BF16).reshape(NSUPER, SLOTS, 256)
            )
        return carry

    lax.fori_loop(0, CH // 256, front_cols, 0)

    frames = front.reshape(FRAMES, SLOTS, CH)

    edge = jnp.zeros((2, SLOTS, CH), BF16)
    wide[0:2] = edge
    wide[FRAMES + 2 : FRAMES + 4] = edge

    def expand_rows(c, carry):
        f0 = c * mb
        rows = frames[pl.ds(f0, mb)].reshape(mb * SLOTS, CH)
        for n in range(CH // 256):
            cols = slice(n * 256, (n + 1) * 256)
            out = jnp.maximum(dot(rows, expand_w[:, cols]), 0.0).astype(BF16)
            out = out.reshape(mb, SLOTS, 256)
            wide[pl.ds(f0 + 2, mb), :, cols] = out
            if n == 0:
                joined[pl.ds(f0, mb), :, :BR] = out[:, :, :BR]
        return carry

    lax.fori_loop(0, FRAMES // mb, expand_rows, 0)

    quads = wide.reshape(FRAMES // 4 + 1, 4, SLOTS, CH)
    outs = joined.reshape(FRAMES // 4, 4, SLOTS, CH)
    bc = FRAMES // 8

    def branch(i, last):
        cols = pl.ds(pl.multiple_of(i * BR, BR), BR)
        after = pl.ds(pl.multiple_of((i + 1) * BR, BR), BR)
        weight = pair_w[i - 1]
        for half in range(2):
            for p in range(2):
                b0 = half * bc
                rows = jnp.concatenate(
                    [
                        quads[b0 : b0 + bc, p, :, cols],
                        quads[b0 : b0 + bc, p + 2, :, cols],
                        quads[b0 + 1 : b0 + 1 + bc, p, :, cols],
                        quads[b0 + 1 : b0 + 1 + bc, p + 2, :, cols],
                    ],
                    axis=2,
                ).reshape(bc * SLOTS, 4 * BR)
                out = jnp.maximum(dot(rows, weight), 0.0).astype(BF16)
                out = out.reshape(bc, SLOTS, 2 * BR)
                early, late = out[:, :, :BR], out[:, :, BR:]
                outs[b0 : b0 + bc, p, :, cols] = early
                outs[b0 : b0 + bc, p + 2, :, cols] = late
                if not last:
                    at = quads[b0 : b0 + bc, p + 2, :, after]
                    quads[b0 : b0 + bc, p + 2, :, after] = at + early
                    at = quads[b0 + 1 : b0 + 1 + bc, p, :, after]
                    quads[b0 + 1 : b0 + 1 + bc, p, :, after] = at + late

    def branch_step(i, carry):
        branch(i, False)
        return carry

    lax.fori_loop(1, SCALE - 1, branch_step, 0)
    branch(SCALE - 1, True)

    total[...] = jnp.zeros_like(total)

    def merge_rows(c, carry):
        f0 = c * mb
        rows = joined[pl.ds(f0, mb)].reshape(mb * SLOTS, CH)
        for n in range(CH // 256):
            cols = slice(n * 256, (n + 1) * 256)
            out = jnp.maximum(dot(rows, merge_w[:, cols]), 0.0).reshape(mb, SLOTS, 256)
            merged[pl.ds(f0, mb), :, cols] = out
            total[:, cols] += jnp.sum(out, axis=0)
        return carry

    lax.fori_loop(0, FRAMES // mb, merge_rows, 0)

    squeezed = total[...] * (1.0 / FRAMES)
    hidden = jnp.maximum(exact_dot(squeezed, squeeze_w[...]), 0.0)
    total[...] = jax.nn.sigmoid(exact_dot(hidden, excite_w[...]))

    first[...] = jnp.zeros_like(first)
    second[...] = jnp.zeros_like(second)
    third[...] = (
        (frames[0].astype(F32) + merged[0] * total[...]).astype(BF16).astype(F32)
    )

    def trunk_rows(c, carry):
        f0 = c * mb
        acc = jnp.zeros((mb * SLOTS, ATT), F32)
        for n in range(CH // 256):
            cols = slice(n * 256, (n + 1) * 256)
            out = (
                frames[pl.ds(f0, mb), :, cols].astype(F32)
                + merged[pl.ds(f0, mb), :, cols] * total[:, cols][None]
            ).astype(BF16)
            frames[pl.ds(f0, mb), :, cols] = out
            off = out.astype(F32) - third[:, cols][None]
            first[:, cols] += jnp.sum(off, axis=0)
            second[:, cols] += jnp.sum(off * off, axis=0)
            acc = acc + dot(out.reshape(mb * SLOTS, 256), attend_w[cols, :])
        pre[pl.ds(f0, mb)] = acc.reshape(mb, SLOTS, ATT)
        return carry

    lax.fori_loop(0, FRAMES // mb, trunk_rows, 0)

    drift = first[...] * (1.0 / FRAMES)
    center = third[...] + drift
    variance = jnp.maximum(second[...] * (1.0 / FRAMES) - drift * drift, 0.0)
    spread = jnp.sqrt(variance + EPS_STAT)
    context = exact_dot(center, attend_w[CH : 2 * CH]) + exact_dot(spread, attend_w[2 * CH :])
    attended[...] = jnp.tanh(pre[...] + context[None]).astype(BF16)

    third[...] = center
    total[...] = 1.0 / spread
    pooled_mean, pooled_dev = [], []
    for n in range(CH // 256):
        cols = slice(n * 256, (n + 1) * 256)
        shift = third[:, cols]
        scale = total[:, cols]

        def pool_rows(c, carry, cols=cols, shift=shift, scale=scale):
            s0, s1, s2 = carry
            f0 = c * mb
            rows = attended[pl.ds(f0, mb)].reshape(mb * SLOTS, ATT)
            energy = dot(rows, score_w[:, cols]).reshape(mb, SLOTS, 256)
            weight = jnp.exp(energy)
            z = (frames[pl.ds(f0, mb), :, cols].astype(F32) - shift[None]) * scale[None]
            wz = weight * z
            s0 = s0 + jnp.sum(weight, axis=0)
            s1 = s1 + jnp.sum(wz, axis=0)
            s2 = s2 + jnp.sum(wz * z, axis=0)
            return s0, s1, s2

        zero = jnp.zeros((SLOTS, 256), F32)
        s0, s1, s2 = lax.fori_loop(0, FRAMES // mb, pool_rows, (zero, zero, zero))
        m1 = s1 / s0
        m2 = jnp.maximum(s2 / s0 - m1 * m1, 0.0)
        dev = 1.0 / scale
        pooled_mean.append(shift + m1 * dev)
        pooled_dev.append(jnp.sqrt(m2 * dev * dev + EPS_STAT))
    pooled = jnp.concatenate(pooled_mean + pooled_dev, axis=1).astype(BF16)
    embedding = dot(pooled, embed_w[...])
    logits = dot(embedding.astype(BF16), lang_w[...])
    mean_square = jnp.mean(jnp.square(embedding), axis=1, keepdims=True)
    normed = (embedding * lax.rsqrt(mean_square + EPS_NORM)).astype(BF16).astype(F32)
    parts = [
        normed[:, :LANES],
        jnp.concatenate([normed[:, LANES:], jnp.zeros((SLOTS, 2 * LANES - EMB), F32)], axis=1),
        jnp.concatenate([logits, jnp.zeros((SLOTS, LANES - LANGS), F32)], axis=1),
        header,
    ]
    for k, part in enumerate(parts):
        for m in range(8):
            out_ref[:, m, k, :] = part


def family(recv, weights):
    vmem = pl.BlockSpec(memory_space=pltpu.VMEM)
    return pl.pallas_call(
        family_kernel,
        out_shape=jax.ShapeDtypeStruct((SLOTS, 8, 4, LANES), F32),
        in_specs=[vmem] * (1 + len(weights)),
        out_specs=vmem,
        scratch_shapes=[
            pltpu.VMEM((ROWS, SLOTS, LANES), F32),
            pltpu.VMEM((NSUPER + 2, SLOTS, WIDE), BF16),
            pltpu.VMEM((NSUPER, SUPER, SLOTS, CH), BF16),
            pltpu.VMEM((FRAMES + 4, SLOTS, CH), BF16),
            pltpu.VMEM((FRAMES, SLOTS, CH), BF16),
            pltpu.VMEM((FRAMES, SLOTS, CH), F32),
            pltpu.VMEM((FRAMES, SLOTS, ATT), F32),
            pltpu.VMEM((FRAMES, SLOTS, ATT), BF16),
            pltpu.VMEM((SLOTS, CH), F32),
            pltpu.VMEM((SLOTS, CH), F32),
            pltpu.VMEM((SLOTS, CH), F32),
            pltpu.VMEM((SLOTS, CH), F32),
        ],
        compiler_params=pltpu.CompilerParams(vmem_limit_bytes=58 << 20),
        cost_estimate=pl.CostEstimate(
            flops=20_000_000_000, bytes_accessed=10_000_000, transcendentals=4_000_000
        ),
        name="family",
    )(recv, *weights)


def home_kernel(mem_ref, recv_ref, logits_ref, sim_ref, held):
    head0, head1 = recv_ref[:, 0, :], recv_ref[:, 1, :]
    mark = recv_ref[:, 3, :]
    rows = recv_ref.shape[0]
    row = lax.broadcasted_iota(jnp.int32, (rows, LANES), 0)
    lane = lax.broadcasted_iota(jnp.int32, (rows, LANES), 1)
    place = lax.rem(row, 8) * STORE + mark.astype(jnp.int32) - 1
    pick = jnp.where((mark > 0.5) & (place == lane), 1.0, 0.0)
    pick16 = pick.astype(BF16)
    turned = (((0,), (0,)), ((), ()))
    normed = lax.dot_general(
        pick16,
        jnp.concatenate([head0, head1], axis=1).astype(BF16),
        turned,
        preferred_element_type=F32,
    )
    held[:, : 2 * LANES] = normed
    held[:, 2 * LANES :] = lax.dot_general(
        pick, recv_ref[:, 2, :], turned, preferred_element_type=F32, precision=lax.Precision.HIGHEST
    )
    own = held[pl.ds(pl.multiple_of(mem_ref[0] * STORE, STORE), STORE)]
    logits_ref[0] = own[:, 2 * LANES : 2 * LANES + LANGS]
    sim = lax.dot_general(
        own[:, : 2 * LANES].astype(BF16),
        normed[: 8 * STORE].astype(BF16),
        (((1,), (1,)), ((), ())),
        preferred_element_type=F32,
    )
    sim_ref[0] = sim / EMB


def home(member, recv):
    vmem = pl.BlockSpec(memory_space=pltpu.VMEM)
    return pl.pallas_call(
        home_kernel,
        out_shape=(
            jax.ShapeDtypeStruct((1, STORE, LANGS), F32),
            jax.ShapeDtypeStruct((1, STORE, 8 * STORE), F32),
        ),
        in_specs=[pl.BlockSpec(memory_space=pltpu.SMEM), vmem],
        out_specs=(vmem, vmem),
        scratch_shapes=[pltpu.VMEM((LANES, 3 * LANES), F32)],
        name="home",
    )(member, recv)


def prepare(initial_conv_weight, branch_weight):
    tall = jnp.pad(initial_conv_weight, ((PAD_TOP, PAD_TOP), (0, 0)))
    early = jnp.pad(branch_weight, ((0, 0), (0, BR), (0, 0)))
    late = jnp.pad(branch_weight, ((0, 0), (BR, 0), (0, 0)))
    return tall, jnp.concatenate([early, late], axis=2)


def shards(
    filterbank,
    destination,
    initial_conv_weight,
    expand_weight,
    branch_weight,
    merge_weight,
    squeeze_weight,
    excite_weight,
    attend_weight,
    score_weight,
    embed_weight,
    language_weight,
):
    bank = filterbank.reshape(STORE, FLAT, LANES).transpose(1, 0, 2)
    outbound = pack(bank, destination.reshape(STORE))
    arrived = lax.all_to_all(outbound, "grp", split_axis=0, concat_axis=0, tiled=True)
    tall, pairs = prepare(initial_conv_weight, branch_weight)
    scored = family(
        arrived,
        (
            tall,
            expand_weight,
            pairs,
            merge_weight,
            squeeze_weight,
            excite_weight,
            attend_weight[0],
            score_weight[0],
            embed_weight[0],
            language_weight[0],
        ),
    )
    back = lax.all_to_all(
        scored.reshape(SLOTS * 8, 4, LANES),
        ("grp", "mem"),
        split_axis=0,
        concat_axis=0,
        tiled=True,
    )
    member = lax.axis_index("mem").astype(jnp.int32).reshape(1)
    return home(member, back)


def solution(mesh):
    return jax.shard_map(
        shards,
        mesh=mesh,
        in_specs=(
            P("grp", "mem", None, None),
            P("grp", "mem"),
            P(),
            P(),
            P(),
            P(),
            P(),
            P(),
            P("grp", None, None),
            P("grp", None, None),
            P("grp", None, None),
            P("grp", None, None),
        ),
        out_specs=(P("grp", "mem", None), P("grp", "mem", None)),
        check_vma=False,
    )
```

```python
import functools

import jax
import jax.numpy as jnp
from jax import lax
from jax.experimental import pallas as pl
from jax.experimental.pallas import tpu as pltpu
from jax.sharding import PartitionSpec as P

MELS = 80
CH = 1024
BR = 128
SCALE = 8
ATT = 128
EMB = 192
LANGS = 107
FRAMES = 200
STORE = 8
SLOTS = 16
LANES = 128

FLAT = FRAMES * MELS // LANES
ROWS = 128

SUPER = 8
NSUPER = FRAMES // SUPER
WIDE = SUPER * MELS
BLOCKS = WIDE // LANES
TAPS = 5 * MELS
PAD_TOP = 112

EPS_STAT = 1e-05
EPS_NORM = 1e-06

F32 = jnp.float32
BF16 = jnp.bfloat16


def dot(a, b):
    return jnp.dot(a, b, preferred_element_type=F32)


def exact_dot(a, b):
    rows = a.shape[0]
    high = a.astype(BF16)
    rest = a - high.astype(F32)
    mid = rest.astype(BF16)
    low = (rest - mid.astype(F32)).astype(BF16)
    out = dot(jnp.concatenate([high, mid, low], axis=0), b)
    return out[:rows] + (out[rows : 2 * rows] + out[2 * rows :])


def pack_kernel(dest_ref, bank_ref, out_ref, row_ref):
    out_ref[...] = jnp.zeros_like(out_ref)
    row_ref[FLAT:] = jnp.zeros((ROWS - FLAT, LANES), F32)
    for s in range(STORE):
        row_ref[:FLAT] = bank_ref[pl.ds(s, FLAT, stride=STORE), :]
        row_ref[FLAT:] = jnp.full((ROWS - FLAT, LANES), s + 1, F32)
        out_ref[dest_ref[s]] = row_ref[...].astype(BF16)


def pack(bank, dest):
    return pl.pallas_call(
        pack_kernel,
        out_shape=jax.ShapeDtypeStruct((SLOTS, ROWS, LANES), BF16),
        in_specs=[
            pl.BlockSpec(memory_space=pltpu.SMEM),
            pl.BlockSpec(memory_space=pltpu.VMEM),
        ],
        out_specs=pl.BlockSpec(memory_space=pltpu.VMEM),
        scratch_shapes=[pltpu.VMEM((ROWS, LANES), F32)],
        name="pack",
    )(dest, bank)


def slot_sums(values):
    frames, slots, columns = values.shape
    row = lax.broadcasted_iota(jnp.int32, (slots, frames * slots), 0)
    column = lax.broadcasted_iota(jnp.int32, (slots, frames * slots), 1)
    same = jnp.where(lax.rem(column, slots) == row, 1.0, 0.0).astype(BF16)
    return dot(same, values.reshape(frames * slots, columns))


def family_kernel(
    recv_ref,
    front_h,
    expand_h,
    pair_h,
    merge_h,
    squeeze_h,
    excite_h,
    attend_h,
    score_h,
    embed_h,
    lang_h,
    out_ref,
    front_w,
    expand_w,
    pair_w,
    merge_w,
    squeeze_w,
    excite_w,
    attend_w,
    score_w,
    embed_w,
    lang_w,
    sems,
    flat,
    bank,
    front,
    wide,
    joined,
    merged,
    pre,
    attended,
    total,
    first,
    second,
):
    mb = 40
    nb = 256
    copies = [
        pltpu.make_async_copy(source, target, sems.at[i])
        for i, (source, target) in enumerate(
            [
                (front_h, front_w),
                (expand_h, expand_w),
                (pair_h, pair_w),
                (merge_h, merge_w),
                (squeeze_h, squeeze_w),
                (excite_h, excite_w),
                (attend_h, attend_w),
                (score_h, score_w),
                (embed_h, embed_w),
                (lang_h, lang_w),
            ]
        )
    ]
    for copy in copies:
        copy.start()

    for s in range(SLOTS):
        flat[pl.ds(s, ROWS, stride=SLOTS), :] = recv_ref[s].astype(F32)
    header = flat[FLAT * SLOTS : (FLAT + 1) * SLOTS]
    bank[0] = jnp.zeros((SLOTS, WIDE), BF16)
    bank[NSUPER + 1] = jnp.zeros((SLOTS, WIDE), BF16)
    for r in range(NSUPER):
        for t in range(BLOCKS):
            at = (BLOCKS * r + t) * SLOTS
            bank[r + 1, :, t * LANES : (t + 1) * LANES] = flat[at : at + SLOTS].astype(BF16)

    copies[0].wait()

    def front_cols(n, carry):
        cols = pl.ds(pl.multiple_of(n * nb, nb), nb)
        sums = jnp.zeros((SLOTS, nb), F32)
        for j in range(SUPER):
            start = MELS * (j - 2)
            block, offset = start // LANES, start % LANES
            pieces = []
            for t in range(block, block + 4):
                shift, lane = t // BLOCKS, t % BLOCKS
                pieces.append(
                    bank[1 + shift : 1 + shift + NSUPER, :, lane * LANES : (lane + 1) * LANES]
                )
            window = jnp.concatenate(pieces, axis=2).reshape(NSUPER * SLOTS, 4 * LANES)
            top = PAD_TOP - offset
            out = dot(window, front_w[top : top + 4 * LANES, cols])
            out = jnp.maximum(out.astype(BF16), 0.0).reshape(NSUPER, SLOTS, nb)
            front[:, j, :, cols] = out
            sums = sums + slot_sums(out)
        first[:, cols] = sums
        return carry

    lax.fori_loop(0, CH // nb, front_cols, 0)

    frames = front.reshape(FRAMES, SLOTS, CH)

    copies[1].wait()
    edge = jnp.zeros((2, SLOTS, CH), BF16)
    wide[0:2] = edge
    wide[FRAMES + 2 : FRAMES + 4] = edge

    def expand_rows(c, carry):
        f0 = c * mb
        rows = frames[pl.ds(f0, mb)].reshape(mb * SLOTS, CH)
        for n in range(CH // nb):
            cols = slice(n * nb, (n + 1) * nb)
            out = jnp.maximum(dot(rows, expand_w[:, cols]).astype(BF16), 0.0)
            out = out.reshape(mb, SLOTS, nb)
            wide[pl.ds(f0 + 2, mb), :, cols] = out
            if n == 0:
                joined[pl.ds(f0, mb), :, :BR] = out[:, :, :BR]
        return carry

    lax.fori_loop(0, FRAMES // mb, expand_rows, 0)

    copies[2].wait()
    quads = wide.reshape(FRAMES // 4 + 1, 4, SLOTS, CH)
    outs = joined.reshape(FRAMES // 4, 4, SLOTS, CH)
    nq = FRAMES // 4
    for i in range(1, SCALE):
        cols = slice(i * BR, (i + 1) * BR)
        after = slice((i + 1) * BR, (i + 2) * BR)
        rows = jnp.concatenate(
            [
                jnp.concatenate(
                    [
                        quads[:nq, p, :, cols],
                        quads[:nq, p + 2, :, cols],
                        quads[1:, p, :, cols],
                        quads[1:, p + 2, :, cols],
                    ],
                    axis=2,
                )
                for p in range(2)
            ],
            axis=0,
        ).reshape(2 * nq * SLOTS, 4 * BR)
        out = jnp.maximum(dot(rows, pair_w[i - 1]).astype(BF16), 0.0)
        out = out.reshape(2, nq, SLOTS, 2 * BR)
        for p in range(2):
            early, late = out[p, :, :, :BR], out[p, :, :, BR:]
            outs[:, p, :, cols] = early
            outs[:, p + 2, :, cols] = late
            if i < SCALE - 1:
                quads[:nq, p + 2, :, after] = quads[:nq, p + 2, :, after] + early
                quads[1:, p, :, after] = quads[1:, p, :, after] + late

    copies[3].wait()
    total[...] = jnp.zeros_like(total)

    def merge_rows(c, carry):
        f0 = c * mb
        rows = joined[pl.ds(f0, mb)].reshape(mb * SLOTS, CH)
        for n in range(CH // nb):
            cols = slice(n * nb, (n + 1) * nb)
            out = jnp.maximum(dot(rows, merge_w[:, cols]), 0.0).reshape(mb, SLOTS, nb)
            merged[pl.ds(f0, mb), :, cols] = out.astype(BF16)
            total[:, cols] += jnp.sum(out, axis=0)
        return carry

    lax.fori_loop(0, FRAMES // mb, merge_rows, 0)

    for k in range(4, 10):
        copies[k].wait()
    squeezed = total[...] * (1.0 / FRAMES)
    hidden = jnp.maximum(exact_dot(squeezed, squeeze_w[...]), 0.0)
    excited = jax.nn.sigmoid(exact_dot(hidden, excite_w[...]))
    gate = excited.astype(BF16)

    shift = (first[...] * (1.0 / FRAMES) + squeezed * excited).astype(BF16)
    first[...] = jnp.zeros_like(first)
    second[...] = jnp.zeros_like(second)

    def trunk_rows(c, carry):
        f0 = c * mb
        acc = jnp.zeros((mb * SLOTS, ATT), F32)
        for n in range(CH // nb):
            cols = slice(n * nb, (n + 1) * nb)
            out = frames[pl.ds(f0, mb), :, cols] + (
                merged[pl.ds(f0, mb), :, cols] * gate[:, cols][None]
            )
            frames[pl.ds(f0, mb), :, cols] = out
            off = out - shift[:, cols][None]
            first[:, cols] += slot_sums(off)
            second[:, cols] += slot_sums(off * off)
            acc = acc + dot(out.reshape(mb * SLOTS, nb), attend_w[cols, :])
        pre[pl.ds(f0, mb)] = acc.reshape(mb, SLOTS, ATT)
        return carry

    lax.fori_loop(0, FRAMES // mb, trunk_rows, 0)

    drift = first[...] * (1.0 / FRAMES)
    center = shift.astype(F32) + drift
    variance = jnp.maximum(second[...] * (1.0 / FRAMES) - drift * drift, 0.0)
    spread = jnp.sqrt(variance + EPS_STAT)
    context = exact_dot(center, attend_w[CH : 2 * CH]) + exact_dot(spread, attend_w[2 * CH :])
    attended[...] = jnp.tanh(pre[...] + context[None]).astype(BF16)

    first[...] = center
    second[...] = 1.0 / spread

    def pool_cols(n, carry):
        cols = pl.ds(pl.multiple_of(n * nb, nb), nb)
        middle = first[:, cols].astype(BF16)
        scale = second[:, cols].astype(BF16)
        s0 = jnp.zeros((SLOTS, nb), F32)
        s1 = jnp.zeros((SLOTS, nb), F32)
        s2 = jnp.zeros((SLOTS, nb), F32)
        for f0 in range(0, FRAMES, mb):
            rows = attended[f0 : f0 + mb].reshape(mb * SLOTS, ATT)
            energy = dot(rows, score_w[:, cols]).reshape(mb, SLOTS, nb)
            weight = jnp.exp(energy)
            s0 = s0 + jnp.sum(weight, axis=0)
            z = (frames[f0 : f0 + mb, :, cols] - middle[None]) * scale[None]
            wz = weight.astype(BF16) * z
            s1 = s1 + slot_sums(wz)
            s2 = s2 + slot_sums(wz * z)
        m1 = s1 / s0
        m2 = jnp.maximum(s2 / s0 - m1 * m1, 0.0)
        dev = 1.0 / scale.astype(F32)
        first[:, cols] = middle.astype(F32) + m1 * dev
        second[:, cols] = jnp.sqrt(m2 * dev * dev + EPS_STAT)
        return carry

    lax.fori_loop(0, CH // nb, pool_cols, 0)
    pooled = jnp.concatenate([first[...], second[...]], axis=1).astype(BF16)
    embedding = dot(pooled, embed_w[...])
    logits = dot(embedding.astype(BF16), lang_w[...])
    mean_square = jnp.mean(jnp.square(embedding), axis=1, keepdims=True)
    normed = (embedding * lax.rsqrt(mean_square + EPS_NORM)).astype(BF16).astype(F32)
    parts = [
        normed[:, :LANES],
        jnp.concatenate([normed[:, LANES:], jnp.zeros((SLOTS, 2 * LANES - EMB), F32)], axis=1),
        jnp.concatenate([logits, jnp.zeros((SLOTS, LANES - LANGS), F32)], axis=1),
        header,
    ]
    for k, part in enumerate(parts):
        for m in range(8):
            out_ref[pl.ds(4 * m + k, SLOTS, stride=32), :] = part


def family(recv, weights):
    vmem = pl.BlockSpec(memory_space=pltpu.VMEM)
    away = pl.BlockSpec(memory_space=pl.ANY)
    return pl.pallas_call(
        family_kernel,
        out_shape=jax.ShapeDtypeStruct((SLOTS * 8 * 4, LANES), F32),
        in_specs=[vmem] + [away] * len(weights),
        out_specs=vmem,
        scratch_shapes=[pltpu.VMEM(w.shape, w.dtype) for w in weights]
        + [
            pltpu.SemaphoreType.DMA((len(weights),)),
            pltpu.VMEM((ROWS * SLOTS, LANES), F32),
            pltpu.VMEM((NSUPER + 2, SLOTS, WIDE), BF16),
            pltpu.VMEM((NSUPER, SUPER, SLOTS, CH), BF16),
            pltpu.VMEM((FRAMES + 4, SLOTS, CH), BF16),
            pltpu.VMEM((FRAMES, SLOTS, CH), BF16),
            pltpu.VMEM((FRAMES, SLOTS, CH), BF16),
            pltpu.VMEM((FRAMES, SLOTS, ATT), F32),
            pltpu.VMEM((FRAMES, SLOTS, ATT), BF16),
            pltpu.VMEM((SLOTS, CH), F32),
            pltpu.VMEM((SLOTS, CH), F32),
            pltpu.VMEM((SLOTS, CH), F32),
        ],
        compiler_params=pltpu.CompilerParams(vmem_limit_bytes=52 << 20),
        cost_estimate=pl.CostEstimate(
            flops=20_000_000_000, bytes_accessed=10_000_000, transcendentals=4_000_000
        ),
        name="family",
    )(recv, *weights)


def home_kernel(mem_ref, recv_ref, logits_ref, sim_ref, held):
    rows = recv_ref.shape[0] // 4
    head0, head1, tail, mark = (recv_ref[pl.ds(k, rows, stride=4), :] for k in range(4))
    row = lax.broadcasted_iota(jnp.int32, (rows, LANES), 0)
    lane = lax.broadcasted_iota(jnp.int32, (rows, LANES), 1)
    place = lax.rem(row, 8) * STORE + mark.astype(jnp.int32) - 1
    pick = jnp.where((mark > 0.5) & (place == lane), 1.0, 0.0)
    pick16 = pick.astype(BF16)
    turned = (((0,), (0,)), ((), ()))
    normed = lax.dot_general(
        pick16,
        jnp.concatenate([head0, head1], axis=1).astype(BF16),
        turned,
        preferred_element_type=F32,
    )
    held[:, : 2 * LANES] = normed
    held[:, 2 * LANES :] = lax.dot_general(
        pick, tail, turned, preferred_element_type=F32, precision=lax.Precision.HIGHEST
    )
    own = held[pl.ds(pl.multiple_of(mem_ref[0] * STORE, STORE), STORE)]
    logits_ref[0] = own[:, 2 * LANES : 2 * LANES + LANGS]
    sim = lax.dot_general(
        own[:, : 2 * LANES].astype(BF16),
        normed[: 8 * STORE].astype(BF16),
        (((1,), (1,)), ((), ())),
        preferred_element_type=F32,
    )
    sim_ref[0] = sim / EMB


def home(member, recv):
    vmem = pl.BlockSpec(memory_space=pltpu.VMEM)
    return pl.pallas_call(
        home_kernel,
        out_shape=(
            jax.ShapeDtypeStruct((1, STORE, LANGS), F32),
            jax.ShapeDtypeStruct((1, STORE, 8 * STORE), F32),
        ),
        in_specs=[pl.BlockSpec(memory_space=pltpu.SMEM), vmem],
        out_specs=(vmem, vmem),
        scratch_shapes=[pltpu.VMEM((LANES, 3 * LANES), F32)],
        name="home",
    )(member, recv)


def prepare(initial_conv_weight, branch_weight):
    tall = jnp.pad(initial_conv_weight, ((PAD_TOP, PAD_TOP), (0, 0)))
    early = jnp.pad(branch_weight, ((0, 0), (0, BR), (0, 0)))
    late = jnp.pad(branch_weight, ((0, 0), (BR, 0), (0, 0)))
    return tall, jnp.concatenate([early, late], axis=2)


def shards(
    filterbank,
    destination,
    initial_conv_weight,
    expand_weight,
    branch_weight,
    merge_weight,
    squeeze_weight,
    excite_weight,
    attend_weight,
    score_weight,
    embed_weight,
    language_weight,
):
    bank = filterbank.reshape(STORE, FLAT, LANES).transpose(1, 0, 2).reshape(FLAT * STORE, LANES)
    outbound = pack(bank, destination.reshape(STORE))
    arrived = lax.all_to_all(outbound, "grp", split_axis=0, concat_axis=0, tiled=True)
    tall, pairs = prepare(initial_conv_weight, branch_weight)
    scored = family(
        arrived,
        (
            tall,
            expand_weight,
            pairs,
            merge_weight,
            squeeze_weight,
            excite_weight,
            attend_weight[0],
            score_weight[0],
            embed_weight[0],
            language_weight[0],
        ),
    )
    back = lax.all_to_all(
        scored.reshape(SLOTS * 8, 4, LANES),
        ("grp", "mem"),
        split_axis=0,
        concat_axis=0,
        tiled=True,
    )
    member = lax.axis_index("mem").astype(jnp.int32).reshape(1)
    return home(member, back.reshape(SLOTS * 8 * 4, LANES))


def solution(mesh):
    return jax.shard_map(
        shards,
        mesh=mesh,
        in_specs=(
            P("grp", "mem", None, None),
            P("grp", "mem"),
            P(),
            P(),
            P(),
            P(),
            P(),
            P(),
            P("grp", None, None),
            P("grp", None, None),
            P("grp", None, None),
            P("grp", None, None),
        ),
        out_specs=(P("grp", "mem", None), P("grp", "mem", None)),
        check_vma=False,
    )
```

```python
import functools

import jax
import jax.numpy as jnp
from jax import lax
from jax.experimental import pallas as pl
from jax.experimental.pallas import tpu as pltpu
from jax.sharding import PartitionSpec as P

MELS = 80
CH = 1024
BR = 128
SCALE = 8
ATT = 128
EMB = 192
LANGS = 107
FRAMES = 200
STORE = 8
SLOTS = 16
LANES = 128

FLAT = FRAMES * MELS // LANES
ROWS = 128

SUPER = 8
NSUPER = FRAMES // SUPER
WIDE = SUPER * MELS
BLOCKS = WIDE // LANES
TAPS = 5 * MELS
PAD_TOP = 112

EPS_STAT = 1e-05
EPS_NORM = 1e-06

F32 = jnp.float32
BF16 = jnp.bfloat16


def dot(a, b):
    return jnp.dot(a, b, preferred_element_type=F32)


def exact_dot(a, b):
    rows = a.shape[0]
    high = a.astype(BF16)
    rest = a - high.astype(F32)
    mid = rest.astype(BF16)
    low = (rest - mid.astype(F32)).astype(BF16)
    out = dot(jnp.concatenate([high, mid, low], axis=0), b)
    return out[:rows] + (out[rows : 2 * rows] + out[2 * rows :])


def pack_kernel(dest_ref, bank_ref, out_ref, row_ref):
    out_ref[...] = jnp.zeros_like(out_ref)
    row_ref[FLAT:] = jnp.zeros((ROWS - FLAT, LANES), F32)
    for s in range(STORE):
        row_ref[:FLAT] = bank_ref[pl.ds(s, FLAT, stride=STORE), :]
        row_ref[FLAT:] = jnp.full((ROWS - FLAT, LANES), s + 1, F32)
        out_ref[dest_ref[s]] = row_ref[...].astype(BF16)


def pack(bank, dest):
    return pl.pallas_call(
        pack_kernel,
        out_shape=jax.ShapeDtypeStruct((SLOTS, ROWS, LANES), BF16),
        in_specs=[
            pl.BlockSpec(memory_space=pltpu.SMEM),
            pl.BlockSpec(memory_space=pltpu.VMEM),
        ],
        out_specs=pl.BlockSpec(memory_space=pltpu.VMEM),
        scratch_shapes=[pltpu.VMEM((ROWS, LANES), F32)],
        compiler_params=pltpu.CompilerParams(vmem_limit_bytes=16 << 20),
        name="pack",
    )(dest, bank)


def slot_sums(values):
    frames, slots, columns = values.shape
    row = lax.broadcasted_iota(jnp.int32, (slots, frames * slots), 0)
    column = lax.broadcasted_iota(jnp.int32, (slots, frames * slots), 1)
    same = jnp.where(lax.rem(column, slots) == row, 1.0, 0.0).astype(BF16)
    return dot(same, values.reshape(frames * slots, columns))


def fours(values):
    frames, slots, columns = values.shape
    split = values.reshape(frames // 4, 4, slots, columns)
    return (split[:, 0] + split[:, 1]) + (split[:, 2] + split[:, 3])


def get(ref, frames, blocks):
    return jnp.concatenate([ref[frames, k] for k in blocks], axis=-1)


def put(ref, frames, blocks, values):
    for i, k in enumerate(blocks):
        ref[frames, k] = values[..., i * LANES : (i + 1) * LANES]


def family_kernel(
    recv_ref,
    front_h,
    expand_h,
    pair_h,
    merge_h,
    squeeze_h,
    excite_h,
    attend_h,
    score_h,
    embed_h,
    lang_h,
    out_ref,
    front_w,
    expand_w,
    pair_w,
    merge_w,
    squeeze_w,
    excite_w,
    attend_w,
    score_w,
    embed_w,
    lang_w,
    sems,
    flat,
    bank,
    front,
    wide,
    joined,
    merged,
    pre,
    attended,
    total,
    first,
    second,
):
    mb = 40
    nb = 256
    copies = [
        pltpu.make_async_copy(source, target, sems.at[i])
        for i, (source, target) in enumerate(
            [
                (front_h, front_w),
                (expand_h, expand_w),
                (pair_h, pair_w),
                (merge_h, merge_w),
                (squeeze_h, squeeze_w),
                (excite_h, excite_w),
                (attend_h, attend_w),
                (score_h, score_w),
                (embed_h, embed_w),
                (lang_h, lang_w),
            ]
        )
    ]
    for copy in copies:
        copy.start()

    for s in range(SLOTS):
        flat[pl.ds(s, ROWS, stride=SLOTS), :] = recv_ref[s].astype(F32)
    header = flat[FLAT * SLOTS : (FLAT + 1) * SLOTS]
    bank[0] = jnp.zeros((BLOCKS, SLOTS, LANES), BF16)
    bank[NSUPER + 1] = jnp.zeros((BLOCKS, SLOTS, LANES), BF16)
    bank[1 : NSUPER + 1] = (
        flat[: FLAT * SLOTS].astype(BF16).reshape(NSUPER, BLOCKS, SLOTS, LANES)
    )

    copies[0].wait()

    nk = nb // LANES

    def front_cols(n, carry):
        cols = pl.ds(pl.multiple_of(n * nb, nb), nb)
        blocks = [n * nk + k for k in range(nk)]
        for j in range(SUPER):
            start = MELS * (j - 2)
            block, offset = start // LANES, start % LANES
            window = jnp.concatenate(
                [
                    bank[1 + t // BLOCKS : 1 + t // BLOCKS + NSUPER, t % BLOCKS]
                    for t in range(block, block + 4)
                ],
                axis=2,
            ).reshape(NSUPER * SLOTS, 4 * LANES)
            top = PAD_TOP - offset
            out = dot(window, front_w[top : top + 4 * LANES, cols])
            if j == 0:
                sample = jnp.maximum(out, 0.0).reshape(NSUPER, SLOTS, nb)
                first[:, cols] = jnp.sum(sample, axis=0) * (1.0 / NSUPER)
            out = jnp.maximum(out.astype(BF16), 0.0).reshape(NSUPER, SLOTS, nb)
            for i, k in enumerate(blocks):
                front[:, j, k] = out[:, :, i * LANES : (i + 1) * LANES]
        return carry

    lax.fori_loop(0, CH // nb, front_cols, 0)

    nf = CH // LANES
    frames = front.reshape(FRAMES, nf, SLOTS, LANES)

    copies[1].wait()
    edge = jnp.zeros((2, nf, SLOTS, LANES), BF16)
    wide[0:2] = edge
    wide[FRAMES + 2 : FRAMES + 4] = edge

    def expand_rows(c, carry):
        f0 = c * mb
        rows = get(frames, pl.ds(f0, mb), range(nf)).reshape(mb * SLOTS, CH)
        for n in range(CH // nb):
            cols = slice(n * nb, (n + 1) * nb)
            out = jnp.maximum(dot(rows, expand_w[:, cols]).astype(BF16), 0.0)
            out = out.reshape(mb, SLOTS, nb)
            put(wide, pl.ds(f0 + 2, mb), range(n * nk, (n + 1) * nk), out)
            if n == 0:
                joined[pl.ds(f0, mb), 0] = out[:, :, :BR]
        return carry

    lax.fori_loop(0, FRAMES // mb, expand_rows, 0)

    copies[2].wait()
    nq = FRAMES // 4
    quads = wide.reshape(nq + 1, 4, nf, SLOTS, LANES)
    outs = joined.reshape(nq, 4, nf, SLOTS, LANES)
    for i in range(1, SCALE):
        cut = nq // 2 + SCALE // 2 - i
        for lo, hi in ((0, cut), (cut, nq)):
            n = hi - lo
            rows = jnp.concatenate(
                [
                    jnp.concatenate(
                        [
                            quads[lo:hi, p, i],
                            quads[lo:hi, p + 2, i],
                            quads[lo + 1 : hi + 1, p, i],
                            quads[lo + 1 : hi + 1, p + 2, i],
                        ],
                        axis=2,
                    )
                    for p in range(2)
                ],
                axis=0,
            ).reshape(2 * n * SLOTS, 4 * BR)
            out = jnp.maximum(dot(rows, pair_w[i - 1]).astype(BF16), 0.0)
            out = out.reshape(2, n, SLOTS, 2 * BR)
            for p in range(2):
                early, late = out[p, :, :, :BR], out[p, :, :, BR:]
                outs[lo:hi, p, i] = early
                outs[lo:hi, p + 2, i] = late
                if i < SCALE - 1:
                    quads[lo:hi, p + 2, i + 1] = quads[lo:hi, p + 2, i + 1] + early
                    quads[lo + 1 : hi + 1, p, i + 1] = quads[lo + 1 : hi + 1, p, i + 1] + late

    copies[3].wait()
    total[...] = jnp.zeros_like(total)

    def merge_rows(c, carry):
        f0 = c * mb
        rows = get(joined, pl.ds(f0, mb), range(nf)).reshape(mb * SLOTS, CH)
        for n in range(CH // nb):
            cols = slice(n * nb, (n + 1) * nb)
            out = jnp.maximum(dot(rows, merge_w[:, cols]), 0.0).reshape(mb, SLOTS, nb)
            put(merged, pl.ds(f0, mb), range(n * nk, (n + 1) * nk), out.astype(BF16))
            total[:, cols] += jnp.sum(out, axis=0)
        return carry

    lax.fori_loop(0, FRAMES // mb, merge_rows, 0)

    for k in range(4, 10):
        copies[k].wait()
    squeezed = total[...] * (1.0 / FRAMES)
    hidden = jnp.maximum(exact_dot(squeezed, squeeze_w[...]), 0.0)
    excited = jax.nn.sigmoid(exact_dot(hidden, excite_w[...]))
    gate = excited.astype(BF16)

    shift = (first[...] + squeezed * excited).astype(BF16)
    first[...] = jnp.zeros_like(first)
    second[...] = jnp.zeros_like(second)

    def trunk_rows(c, carry):
        f0 = c * mb
        acc = jnp.zeros((mb * SLOTS, ATT), F32)
        for n in range(CH // nb):
            cols = slice(n * nb, (n + 1) * nb)
            blocks = range(n * nk, (n + 1) * nk)
            out = get(frames, pl.ds(f0, mb), blocks) + (
                get(merged, pl.ds(f0, mb), blocks) * gate[:, cols][None]
            )
            put(frames, pl.ds(f0, mb), blocks, out)
            off = out - shift[:, cols][None]
            first[:, cols] += slot_sums(fours(off))
            second[:, cols] += slot_sums(fours(off * off))
            acc = acc + dot(out.reshape(mb * SLOTS, nb), attend_w[cols, :])
        pre[pl.ds(f0, mb)] = acc.reshape(mb, SLOTS, ATT)
        return carry

    lax.fori_loop(0, FRAMES // mb, trunk_rows, 0)

    drift = first[...] * (1.0 / FRAMES)
    center = shift.astype(F32) + drift
    variance = jnp.maximum(second[...] * (1.0 / FRAMES) - drift * drift, 0.0)
    spread = jnp.sqrt(variance + EPS_STAT)
    context = exact_dot(center, attend_w[CH : 2 * CH]) + exact_dot(spread, attend_w[2 * CH :])
    attended[...] = jnp.tanh(pre[...] + context[None]).astype(BF16)

    first[...] = center
    second[...] = 1.0 / spread

    for n in range(CH // nb):
        cols = slice(n * nb, (n + 1) * nb)
        blocks = range(n * nk, (n + 1) * nk)
        middle = first[:, cols].astype(BF16)
        scale = second[:, cols].astype(BF16)
        parts = []
        for f0 in range(0, FRAMES, mb):
            rows = attended[f0 : f0 + mb].reshape(mb * SLOTS, ATT)
            energy = dot(rows, score_w[:, cols]).reshape(mb, SLOTS, nb)
            weight = jnp.exp(energy).astype(BF16)
            z = (get(frames, slice(f0, f0 + mb), blocks) - middle[None]) * scale[None]
            wz = weight * z
            parts.append((fours(weight), fours(wz), fours(wz * z)))
        s0, s1, s2 = (slot_sums(jnp.concatenate(part, axis=0)) for part in zip(*parts))
        m1 = s1 / s0
        m2 = jnp.maximum(s2 / s0 - m1 * m1, 0.0)
        dev = 1.0 / scale.astype(F32)
        first[:, cols] = middle.astype(F32) + m1 * dev
        second[:, cols] = jnp.sqrt(m2 * dev * dev + EPS_STAT)
    pooled = jnp.concatenate([first[...], second[...]], axis=1).astype(BF16)
    embedding = dot(pooled, embed_w[...])
    logits = dot(embedding.astype(BF16), lang_w[...])
    mean_square = jnp.mean(jnp.square(embedding), axis=1, keepdims=True)
    normed = (embedding * lax.rsqrt(mean_square + EPS_NORM)).astype(BF16).astype(F32)
    high = logits.astype(BF16).astype(F32)
    fill = jnp.zeros((SLOTS, LANES - LANGS), F32)
    parts = [
        normed[:, :LANES],
        jnp.concatenate([normed[:, LANES:], header[:, : 2 * LANES - EMB]], axis=1),
        jnp.concatenate([high, fill], axis=1),
        jnp.concatenate([logits - high, fill], axis=1),
    ]
    for k, part in enumerate(parts):
        for m in range(8):
            flat[pl.ds(4 * m + k, SLOTS, stride=32), :] = part
    out_ref[...] = flat[: SLOTS * 32].astype(BF16)


def family(recv, weights):
    vmem = pl.BlockSpec(memory_space=pltpu.VMEM)
    away = pl.BlockSpec(memory_space=pl.ANY)
    return pl.pallas_call(
        family_kernel,
        out_shape=jax.ShapeDtypeStruct((SLOTS * 8 * 4, LANES), BF16),
        in_specs=[vmem] + [away] * len(weights),
        out_specs=vmem,
        scratch_shapes=[pltpu.VMEM(w.shape, w.dtype) for w in weights]
        + [
            pltpu.SemaphoreType.DMA((len(weights),)),
            pltpu.VMEM((ROWS * SLOTS, LANES), F32),
            pltpu.VMEM((NSUPER + 2, BLOCKS, SLOTS, LANES), BF16),
            pltpu.VMEM((NSUPER, SUPER, CH // LANES, SLOTS, LANES), BF16),
            pltpu.VMEM((FRAMES + 4, CH // LANES, SLOTS, LANES), BF16),
            pltpu.VMEM((FRAMES, CH // LANES, SLOTS, LANES), BF16),
            pltpu.VMEM((FRAMES, CH // LANES, SLOTS, LANES), BF16),
            pltpu.VMEM((FRAMES, SLOTS, ATT), F32),
            pltpu.VMEM((FRAMES, SLOTS, ATT), BF16),
            pltpu.VMEM((SLOTS, CH), F32),
            pltpu.VMEM((SLOTS, CH), F32),
            pltpu.VMEM((SLOTS, CH), F32),
        ],
        compiler_params=pltpu.CompilerParams(vmem_limit_bytes=52 << 20),
        cost_estimate=pl.CostEstimate(
            flops=20_000_000_000, bytes_accessed=10_000_000, transcendentals=4_000_000
        ),
        name="family",
    )(recv, *weights)


def home_kernel(mem_ref, recv_ref, logits_ref, sim_ref, flat, held):
    rows = recv_ref.shape[0] // 4
    flat[...] = recv_ref[...].astype(F32)
    parts = [flat[pl.ds(k, rows, stride=4), :] for k in range(4)]
    mark = parts[1][:, LANES - 1 :]
    row = lax.broadcasted_iota(jnp.int32, (rows, LANES), 0)
    lane = lax.broadcasted_iota(jnp.int32, (rows, LANES), 1)
    place = lax.rem(row, 8) * STORE + mark.astype(jnp.int32) - 1
    pick = jnp.where((mark > 0.5) & (place == lane), 1.0, 0.0).astype(BF16)
    held[...] = lax.dot_general(
        pick,
        jnp.concatenate(parts, axis=1).astype(BF16),
        (((0,), (0,)), ((), ())),
        preferred_element_type=F32,
    )
    own = held[pl.ds(pl.multiple_of(mem_ref[0] * STORE, STORE), STORE)]
    logits = own[:, 2 * LANES : 3 * LANES] + own[:, 3 * LANES :]
    logits_ref[0] = logits[:, :LANGS]
    sim = lax.dot_general(
        own[:, :EMB].astype(BF16),
        held[: 8 * STORE, :EMB].astype(BF16),
        (((1,), (1,)), ((), ())),
        preferred_element_type=F32,
    )
    sim_ref[0] = sim / EMB


def home(member, recv):
    vmem = pl.BlockSpec(memory_space=pltpu.VMEM)
    return pl.pallas_call(
        home_kernel,
        out_shape=(
            jax.ShapeDtypeStruct((1, STORE, LANGS), F32),
            jax.ShapeDtypeStruct((1, STORE, 8 * STORE), F32),
        ),
        in_specs=[pl.BlockSpec(memory_space=pltpu.SMEM), vmem],
        out_specs=(vmem, vmem),
        scratch_shapes=[
            pltpu.VMEM(recv.shape, F32),
            pltpu.VMEM((LANES, 4 * LANES), F32),
        ],
        compiler_params=pltpu.CompilerParams(vmem_limit_bytes=16 << 20),
        name="home",
    )(member, recv)


def prepare(initial_conv_weight, branch_weight):
    tall = jnp.pad(initial_conv_weight, ((PAD_TOP, PAD_TOP), (0, 0)))
    early = jnp.pad(branch_weight, ((0, 0), (0, BR), (0, 0)))
    late = jnp.pad(branch_weight, ((0, 0), (BR, 0), (0, 0)))
    return tall, jnp.concatenate([early, late], axis=2)


def shards(
    filterbank,
    destination,
    initial_conv_weight,
    expand_weight,
    branch_weight,
    merge_weight,
    squeeze_weight,
    excite_weight,
    attend_weight,
    score_weight,
    embed_weight,
    language_weight,
):
    bank = filterbank.reshape(STORE, FLAT, LANES).transpose(1, 0, 2).reshape(FLAT * STORE, LANES)
    outbound = pack(bank, destination.reshape(STORE))
    arrived = lax.all_to_all(outbound, "grp", split_axis=0, concat_axis=0, tiled=True)
    tall, pairs = prepare(initial_conv_weight, branch_weight)
    scored = family(
        arrived,
        (
            tall,
            expand_weight,
            pairs,
            merge_weight,
            squeeze_weight,
            excite_weight,
            attend_weight[0],
            score_weight[0],
            embed_weight[0],
            language_weight[0],
        ),
    )
    back = lax.all_to_all(
        scored.reshape(SLOTS * 8, 4, LANES),
        ("grp", "mem"),
        split_axis=0,
        concat_axis=0,
        tiled=True,
    )
    member = lax.axis_index("mem").astype(jnp.int32).reshape(1)
    return home(member, back.reshape(SLOTS * 8 * 4, LANES))


def solution(mesh):
    return jax.shard_map(
        shards,
        mesh=mesh,
        in_specs=(
            P("grp", "mem", None, None),
            P("grp", "mem"),
            P(),
            P(),
            P(),
            P(),
            P(),
            P(),
            P("grp", None, None),
            P("grp", None, None),
            P("grp", None, None),
            P("grp", None, None),
        ),
        out_specs=(P("grp", "mem", None), P("grp", "mem", None)),
        check_vma=False,
    )
```

```python
import functools

import jax
import jax.numpy as jnp
from jax import lax
from jax.experimental import pallas as pl
from jax.experimental.pallas import tpu as pltpu
from jax.sharding import PartitionSpec as P

MELS = 80
CH = 1024
BR = 128
SCALE = 8
ATT = 128
EMB = 192
LANGS = 107
FRAMES = 200
STORE = 8
SLOTS = 16
LANES = 128

FLAT = FRAMES * MELS // LANES
ROWS = 128

SUPER = 8
NSUPER = FRAMES // SUPER
WIDE = SUPER * MELS
BLOCKS = WIDE // LANES
TAPS = 5 * MELS
PAD_TOP = 112

EPS_STAT = 1e-05
EPS_NORM = 1e-06

LOG2E = 1.4426950408889634

F32 = jnp.float32
BF16 = jnp.bfloat16


def dot(a, b):
    return jnp.dot(a, b, preferred_element_type=F32)


def exact_dot(a, b):
    rows = a.shape[0]
    high = a.astype(BF16)
    rest = a - high.astype(F32)
    mid = rest.astype(BF16)
    low = (rest - mid.astype(F32)).astype(BF16)
    out = dot(jnp.concatenate([high, mid, low], axis=0), b)
    return out[:rows] + (out[rows : 2 * rows] + out[2 * rows :])


def pack_kernel(dest_ref, bank_ref, out_ref, held, rows, sems):
    part = ROWS // 4
    copies = []
    for c in range(4):
        span = pl.ds(c * part * STORE, (min(FLAT, (c + 1) * part) - c * part) * STORE)
        copies.append(pltpu.make_async_copy(bank_ref.at[span], held.at[span], sems.at[c]))
    for copy in copies:
        copy.start()
    out_ref[...] = jnp.zeros_like(out_ref)
    for c in range(4):
        copies[c].wait()
        filled = min(FLAT, (c + 1) * part) - c * part
        for s in range(STORE):
            values = held[pl.ds(c * part * STORE + s, filled, stride=STORE), :]
            if filled < part:
                rows[s, :filled] = values
                rows[s, filled:] = jnp.full((part - filled, LANES), s + 1, F32)
                values = rows[s]
            out_ref[dest_ref[s], c * part : (c + 1) * part] = values.astype(BF16)


def pack(bank, dest):
    return pl.pallas_call(
        pack_kernel,
        out_shape=jax.ShapeDtypeStruct((SLOTS, ROWS, LANES), BF16),
        in_specs=[
            pl.BlockSpec(memory_space=pltpu.SMEM),
            pl.BlockSpec(memory_space=pl.ANY),
        ],
        out_specs=pl.BlockSpec(memory_space=pltpu.VMEM),
        scratch_shapes=[
            pltpu.VMEM((FLAT * STORE, LANES), F32),
            pltpu.VMEM((STORE, ROWS // 4, LANES), F32),
            pltpu.SemaphoreType.DMA((4,)),
        ],
        compiler_params=pltpu.CompilerParams(vmem_limit_bytes=60 << 20),
        name="pack",
    )(dest, bank)


def slot_sums(values):
    frames, slots, columns = values.shape
    row = lax.broadcasted_iota(jnp.int32, (slots, frames * slots), 0)
    column = lax.broadcasted_iota(jnp.int32, (slots, frames * slots), 1)
    same = jnp.where(lax.rem(column, slots) == row, 1.0, 0.0).astype(BF16)
    return dot(same, values.reshape(frames * slots, columns))


def fours(values):
    frames, slots, columns = values.shape
    split = values.reshape(frames // 4, 4, slots, columns)
    return (split[:, 0] + split[:, 1]) + (split[:, 2] + split[:, 3])


def get(ref, frames, blocks):
    return jnp.concatenate([ref[frames, k] for k in blocks], axis=-1)


def put(ref, frames, blocks, values):
    for i, k in enumerate(blocks):
        ref[frames, k] = values[..., i * LANES : (i + 1) * LANES]


def family_kernel(
    recv_ref,
    front_h,
    expand_h,
    pair_h,
    merge_h,
    squeeze_h,
    excite_h,
    attend_h,
    score_h,
    embed_h,
    lang_h,
    out_ref,
    front_w,
    expand_w,
    pair_w,
    merge_w,
    squeeze_w,
    excite_w,
    attend_w,
    score_w,
    embed_w,
    lang_w,
    sems,
    flat,
    bank,
    front,
    wide,
    joined,
    merged,
    pre,
    attended,
    total,
    first,
    second,
):
    wb = 512
    eb, tb, pb = 40, 20, 20
    nb = 256
    copies = [
        pltpu.make_async_copy(source, target, sems.at[i])
        for i, (source, target) in enumerate(
            [
                (front_h, front_w),
                (expand_h, expand_w),
                (pair_h, pair_w),
                (merge_h, merge_w),
                (squeeze_h, squeeze_w),
                (excite_h, excite_w),
                (attend_h, attend_w),
                (score_h, score_w),
                (embed_h, embed_w),
                (lang_h, lang_w),
            ]
        )
    ]
    for copy in copies:
        copy.start()

    for s in range(SLOTS):
        flat[pl.ds(s, ROWS, stride=SLOTS), :] = recv_ref[s].astype(F32)
    header = flat[FLAT * SLOTS : (FLAT + 1) * SLOTS]
    bank[0] = jnp.zeros((BLOCKS, SLOTS, LANES), BF16)
    bank[NSUPER + 1] = jnp.zeros((BLOCKS, SLOTS, LANES), BF16)
    bank[1 : NSUPER + 1] = (
        flat[: FLAT * SLOTS].astype(BF16).reshape(NSUPER, BLOCKS, SLOTS, LANES)
    )

    copies[0].wait()

    nk = nb // LANES

    def front_cols(n, carry):
        cols = pl.ds(pl.multiple_of(n * wb, wb), wb)
        blocks = [n * (wb // LANES) + k for k in range(wb // LANES)]
        for j in range(SUPER):
            start = MELS * (j - 2)
            block, offset = start // LANES, start % LANES
            window = jnp.concatenate(
                [
                    bank[1 + t // BLOCKS : 1 + t // BLOCKS + NSUPER, t % BLOCKS]
                    for t in range(block, block + 4)
                ],
                axis=2,
            ).reshape(NSUPER * SLOTS, 4 * LANES)
            top = PAD_TOP - offset
            out = dot(window, front_w[top : top + 4 * LANES, cols])
            if j == 0:
                sample = jnp.maximum(out, 0.0).reshape(NSUPER, SLOTS, wb)
                first[:, cols] = jnp.sum(sample, axis=0) * (1.0 / NSUPER)
            out = jnp.maximum(out.astype(BF16), 0.0).reshape(NSUPER, SLOTS, wb)
            for i, k in enumerate(blocks):
                front[:, j, k] = out[:, :, i * LANES : (i + 1) * LANES]
        return carry

    lax.fori_loop(0, CH // wb, front_cols, 0)

    nf = CH // LANES
    frames = front.reshape(FRAMES, nf, SLOTS, LANES)

    copies[1].wait()
    edge = jnp.zeros((2, nf, SLOTS, LANES), BF16)
    wide[0:2] = edge
    wide[FRAMES + 2 : FRAMES + 4] = edge

    def expand_rows(f0):
        rows = get(frames, slice(f0, f0 + eb), range(nf)).reshape(eb * SLOTS, CH)
        for n in range(CH // nb):
            cols = slice(n * nb, (n + 1) * nb)
            out = jnp.maximum(dot(rows, expand_w[:, cols]).astype(BF16), 0.0)
            out = out.reshape(eb, SLOTS, nb)
            put(wide, slice(f0 + 2, f0 + 2 + eb), range(n * nk, (n + 1) * nk), out)
            if n == 0:
                joined[slice(f0, f0 + eb), 0] = out[:, :, :BR]

    for f0 in range(0, FRAMES, eb):
        expand_rows(f0)

    copies[2].wait()
    nq = FRAMES // 4
    quads = wide.reshape(nq + 1, 4, nf, SLOTS, LANES)
    outs = joined.reshape(nq, 4, nf, SLOTS, LANES)
    for i in range(1, SCALE):
        cut = nq // 2 + SCALE // 2 - i
        for lo, hi in ((0, cut), (cut, nq)):
            n = hi - lo
            rows = jnp.concatenate(
                [
                    jnp.concatenate(
                        [
                            quads[lo:hi, p, i],
                            quads[lo:hi, p + 2, i],
                            quads[lo + 1 : hi + 1, p, i],
                            quads[lo + 1 : hi + 1, p + 2, i],
                        ],
                        axis=2,
                    )
                    for p in range(2)
                ],
                axis=0,
            ).reshape(2 * n * SLOTS, 4 * BR)
            out = jnp.maximum(dot(rows, pair_w[i - 1]).astype(BF16), 0.0)
            out = out.reshape(2, n, SLOTS, 2 * BR)
            for p in range(2):
                early, late = out[p, :, :, :BR], out[p, :, :, BR:]
                outs[lo:hi, p, i] = early
                outs[lo:hi, p + 2, i] = late
                if i < SCALE - 1:
                    quads[lo:hi, p + 2, i + 1] = quads[lo:hi, p + 2, i + 1] + early
                    quads[lo + 1 : hi + 1, p, i + 1] = quads[lo + 1 : hi + 1, p, i + 1] + late

    copies[3].wait()
    total[...] = jnp.zeros_like(total)

    def merge_rows(f0):
        rows = get(joined, slice(f0, f0 + eb), range(nf)).reshape(eb * SLOTS, CH)
        for n in range(CH // nb):
            cols = slice(n * nb, (n + 1) * nb)
            out = jnp.maximum(dot(rows, merge_w[:, cols]), 0.0).reshape(eb, SLOTS, nb)
            put(merged, slice(f0, f0 + eb), range(n * nk, (n + 1) * nk), out.astype(BF16))
            total[:, cols] += jnp.sum(out, axis=0)

    for f0 in range(0, FRAMES, eb):
        merge_rows(f0)

    for k in range(4, 10):
        copies[k].wait()
    squeezed = total[...] * (1.0 / FRAMES)
    hidden = jnp.maximum(exact_dot(squeezed, squeeze_w[...]), 0.0)
    excited = jax.nn.sigmoid(exact_dot(hidden, excite_w[...]))
    gate = excited.astype(BF16)

    shift = (first[...] + squeezed * excited).astype(BF16)
    first[...] = jnp.zeros_like(first)
    second[...] = jnp.zeros_like(second)

    def trunk_rows(f0):
        acc = jnp.zeros((tb * SLOTS, ATT), F32)
        for n in range(CH // nb):
            cols = slice(n * nb, (n + 1) * nb)
            blocks = range(n * nk, (n + 1) * nk)
            out = get(frames, slice(f0, f0 + tb), blocks) + (
                get(merged, slice(f0, f0 + tb), blocks) * gate[:, cols][None]
            )
            put(frames, slice(f0, f0 + tb), blocks, out)
            off = out - shift[:, cols][None]
            first[:, cols] += slot_sums(fours(off))
            second[:, cols] += slot_sums(fours(off * off))
            acc = acc + dot(out.reshape(tb * SLOTS, nb), attend_w[cols, :])
        pre[slice(f0, f0 + tb)] = acc.reshape(tb, SLOTS, ATT)

    for f0 in range(0, FRAMES, tb):
        trunk_rows(f0)

    drift = first[...] * (1.0 / FRAMES)
    center = shift.astype(F32) + drift
    variance = jnp.maximum(second[...] * (1.0 / FRAMES) - drift * drift, 0.0)
    spread = jnp.sqrt(variance + EPS_STAT)
    context = exact_dot(center, attend_w[CH : 2 * CH]) + exact_dot(spread, attend_w[2 * CH :])
    attended[...] = (jnp.tanh(pre[...] + context[None]) * LOG2E).astype(BF16)

    first[...] = center
    second[...] = 1.0 / spread

    for n in range(CH // nb):
        cols = slice(n * nb, (n + 1) * nb)
        blocks = range(n * nk, (n + 1) * nk)
        middle = first[:, cols].astype(BF16)
        scale = second[:, cols].astype(BF16)
        parts = []
        for f0 in range(0, FRAMES, pb):
            rows = attended[f0 : f0 + pb].reshape(pb * SLOTS, ATT)
            energy = dot(rows, score_w[:, cols]).reshape(pb, SLOTS, nb)
            weight = jnp.exp2(energy).astype(BF16)
            z = (get(frames, slice(f0, f0 + pb), blocks) - middle[None]) * scale[None]
            wz = weight * z
            parts.append((fours(weight), fours(wz), fours(wz * z)))
        s0, s1, s2 = (slot_sums(jnp.concatenate(part, axis=0)) for part in zip(*parts))
        m1 = s1 / s0
        m2 = jnp.maximum(s2 / s0 - m1 * m1, 0.0)
        dev = 1.0 / scale.astype(F32)
        first[:, cols] = middle.astype(F32) + m1 * dev
        second[:, cols] = jnp.sqrt(m2 * dev * dev + EPS_STAT)
    pooled = jnp.concatenate([first[...], second[...]], axis=1).astype(BF16)
    embedding = dot(pooled, embed_w[...])
    logits = dot(embedding.astype(BF16), lang_w[...])
    mean_square = jnp.mean(jnp.square(embedding), axis=1, keepdims=True)
    normed = (embedding * lax.rsqrt(mean_square + EPS_NORM)).astype(BF16).astype(F32)
    high = logits.astype(BF16).astype(F32)
    fill = jnp.zeros((SLOTS, LANES - LANGS), F32)
    parts = [
        normed[:, :LANES],
        jnp.concatenate([normed[:, LANES:], header[:, : 2 * LANES - EMB]], axis=1),
        jnp.concatenate([high, fill], axis=1),
        jnp.concatenate([logits - high, fill], axis=1),
    ]
    for k, part in enumerate(parts):
        for m in range(8):
            flat[pl.ds(4 * m + k, SLOTS, stride=32), :] = part
    out_ref[...] = flat[: SLOTS * 32].astype(BF16)


def family(recv, weights):
    vmem = pl.BlockSpec(memory_space=pltpu.VMEM)
    away = pl.BlockSpec(memory_space=pl.ANY)
    return pl.pallas_call(
        family_kernel,
        out_shape=jax.ShapeDtypeStruct((SLOTS * 8 * 4, LANES), BF16),
        in_specs=[vmem] + [away] * len(weights),
        out_specs=vmem,
        scratch_shapes=[pltpu.VMEM(w.shape, w.dtype) for w in weights]
        + [
            pltpu.SemaphoreType.DMA((len(weights),)),
            pltpu.VMEM((ROWS * SLOTS, LANES), F32),
            pltpu.VMEM((NSUPER + 2, BLOCKS, SLOTS, LANES), BF16),
            pltpu.VMEM((NSUPER, SUPER, CH // LANES, SLOTS, LANES), BF16),
            pltpu.VMEM((FRAMES + 4, CH // LANES, SLOTS, LANES), BF16),
            pltpu.VMEM((FRAMES, CH // LANES, SLOTS, LANES), BF16),
            pltpu.VMEM((FRAMES, CH // LANES, SLOTS, LANES), BF16),
            pltpu.VMEM((FRAMES, SLOTS, ATT), F32),
            pltpu.VMEM((FRAMES, SLOTS, ATT), BF16),
            pltpu.VMEM((SLOTS, CH), F32),
            pltpu.VMEM((SLOTS, CH), F32),
            pltpu.VMEM((SLOTS, CH), F32),
        ],
        compiler_params=pltpu.CompilerParams(vmem_limit_bytes=52 << 20),
        cost_estimate=pl.CostEstimate(
            flops=20_000_000_000, bytes_accessed=10_000_000, transcendentals=4_000_000
        ),
        name="family",
    )(recv, *weights)


def home_kernel(mem_ref, recv_ref, logits_ref, sim_ref, flat, held):
    rows = recv_ref.shape[0] // 4
    flat[...] = recv_ref[...].astype(F32)
    parts = [flat[pl.ds(k, rows, stride=4), :] for k in range(4)]
    mark = parts[1][:, LANES - 1 :]
    row = lax.broadcasted_iota(jnp.int32, (rows, LANES), 0)
    lane = lax.broadcasted_iota(jnp.int32, (rows, LANES), 1)
    place = lax.rem(row, 8) * STORE + mark.astype(jnp.int32) - 1
    pick = jnp.where((mark > 0.5) & (place == lane), 1.0, 0.0).astype(BF16)
    held[...] = lax.dot_general(
        pick,
        jnp.concatenate(parts, axis=1).astype(BF16),
        (((0,), (0,)), ((), ())),
        preferred_element_type=F32,
    )
    own = held[pl.ds(pl.multiple_of(mem_ref[0] * STORE, STORE), STORE)]
    logits = own[:, 2 * LANES : 3 * LANES] + own[:, 3 * LANES :]
    logits_ref[0] = logits[:, :LANGS]
    sim = lax.dot_general(
        own[:, :EMB].astype(BF16),
        held[: 8 * STORE, :EMB].astype(BF16),
        (((1,), (1,)), ((), ())),
        preferred_element_type=F32,
    )
    sim_ref[0] = sim / EMB


def home(member, recv):
    vmem = pl.BlockSpec(memory_space=pltpu.VMEM)
    return pl.pallas_call(
        home_kernel,
        out_shape=(
            jax.ShapeDtypeStruct((1, STORE, LANGS), F32),
            jax.ShapeDtypeStruct((1, STORE, 8 * STORE), F32),
        ),
        in_specs=[pl.BlockSpec(memory_space=pltpu.SMEM), vmem],
        out_specs=(vmem, vmem),
        scratch_shapes=[
            pltpu.VMEM(recv.shape, F32),
            pltpu.VMEM((LANES, 4 * LANES), F32),
        ],
        compiler_params=pltpu.CompilerParams(vmem_limit_bytes=16 << 20),
        name="home",
    )(member, recv)


def prepare(initial_conv_weight, branch_weight):
    tall = jnp.pad(initial_conv_weight, ((PAD_TOP, PAD_TOP), (0, 0)))
    early = jnp.pad(branch_weight, ((0, 0), (0, BR), (0, 0)))
    late = jnp.pad(branch_weight, ((0, 0), (BR, 0), (0, 0)))
    return tall, jnp.concatenate([early, late], axis=2)


def shards(
    filterbank,
    destination,
    initial_conv_weight,
    expand_weight,
    branch_weight,
    merge_weight,
    squeeze_weight,
    excite_weight,
    attend_weight,
    score_weight,
    embed_weight,
    language_weight,
):
    bank = filterbank.reshape(STORE, FLAT, LANES).transpose(1, 0, 2)
    bank = bank.reshape(FLAT * STORE, LANES)
    outbound = pack(bank, destination.reshape(STORE))
    arrived = lax.all_to_all(outbound, "grp", split_axis=0, concat_axis=0, tiled=True)
    tall, pairs = prepare(initial_conv_weight, branch_weight)
    scored = family(
        arrived,
        (
            tall,
            expand_weight,
            pairs,
            merge_weight,
            squeeze_weight,
            excite_weight,
            attend_weight[0],
            score_weight[0],
            embed_weight[0],
            language_weight[0],
        ),
    )
    back = lax.all_to_all(
        scored.reshape(SLOTS * 8, 4, LANES),
        ("grp", "mem"),
        split_axis=0,
        concat_axis=0,
        tiled=True,
    )
    member = lax.axis_index("mem").astype(jnp.int32).reshape(1)
    return home(member, back.reshape(SLOTS * 8 * 4, LANES))


def solution(mesh):
    return jax.shard_map(
        shards,
        mesh=mesh,
        in_specs=(
            P("grp", "mem", None, None),
            P("grp", "mem"),
            P(),
            P(),
            P(),
            P(),
            P(),
            P(),
            P("grp", None, None),
            P("grp", None, None),
            P("grp", None, None),
            P("grp", None, None),
        ),
        out_specs=(P("grp", "mem", None), P("grp", "mem", None)),
        check_vma=False,
    )
```

```python
import functools

import jax
import jax.numpy as jnp
from jax import lax
from jax.experimental import pallas as pl
from jax.experimental.pallas import tpu as pltpu
from jax.sharding import PartitionSpec as P

MELS = 80
CH = 1024
BR = 128
SCALE = 8
ATT = 128
EMB = 192
LANGS = 107
FRAMES = 200
STORE = 8
SLOTS = 16
LANES = 128

FLAT = FRAMES * MELS // LANES
ROWS = 128

SUPER = 8
NSUPER = FRAMES // SUPER
WIDE = SUPER * MELS
BLOCKS = WIDE // LANES
TAPS = 5 * MELS
PAD_TOP = 112

EPS_STAT = 1e-05
EPS_NORM = 1e-06

LOG2E = 1.4426950408889634

F32 = jnp.float32
BF16 = jnp.bfloat16


def dot(a, b):
    return jnp.dot(a, b, preferred_element_type=F32)


def exact_dot(a, b):
    rows = a.shape[0]
    high = a.astype(BF16)
    rest = a - high.astype(F32)
    mid = rest.astype(BF16)
    low = (rest - mid.astype(F32)).astype(BF16)
    out = dot(jnp.concatenate([high, mid, low], axis=0), b)
    return out[:rows] + (out[rows : 2 * rows] + out[2 * rows :])


def pack_kernel(dest_ref, bank_ref, out_ref, row_ref):
    out_ref[...] = jnp.zeros_like(out_ref)
    for s in range(STORE):
        row_ref[:FLAT] = bank_ref[pl.ds(s, FLAT, stride=STORE), :]
        row_ref[FLAT:] = jnp.full((ROWS - FLAT, LANES), s + 1, F32)
        out_ref[dest_ref[s]] = row_ref[...].astype(BF16)


def pack(bank, dest):
    return pl.pallas_call(
        pack_kernel,
        out_shape=jax.ShapeDtypeStruct((SLOTS, ROWS, LANES), BF16),
        in_specs=[
            pl.BlockSpec(memory_space=pltpu.SMEM),
            pl.BlockSpec(memory_space=pltpu.VMEM),
        ],
        out_specs=pl.BlockSpec(memory_space=pltpu.VMEM),
        scratch_shapes=[pltpu.VMEM((ROWS, LANES), F32)],
        name="pack",
    )(dest, bank)


def slot_sums(values):
    frames, slots, columns = values.shape
    row = lax.broadcasted_iota(jnp.int32, (slots, frames * slots), 0)
    column = lax.broadcasted_iota(jnp.int32, (slots, frames * slots), 1)
    same = jnp.where(lax.rem(column, slots) == row, 1.0, 0.0).astype(BF16)
    return dot(same, values.reshape(frames * slots, columns))


def fours(values):
    frames, slots, columns = values.shape
    split = values.reshape(frames // 4, 4, slots, columns)
    return (split[:, 0] + split[:, 1]) + (split[:, 2] + split[:, 3])


def get(ref, frames, blocks):
    return jnp.concatenate([ref[frames, k] for k in blocks], axis=-1)


def put(ref, frames, blocks, values):
    for i, k in enumerate(blocks):
        ref[frames, k] = values[..., i * LANES : (i + 1) * LANES]


def family_kernel(
    recv_ref,
    front_h,
    expand_h,
    pair_h,
    merge_h,
    squeeze_h,
    excite_h,
    attend_h,
    score_h,
    embed_h,
    lang_h,
    out_ref,
    front_w,
    expand_w,
    pair_w,
    merge_w,
    squeeze_w,
    excite_w,
    attend_w,
    score_w,
    embed_w,
    lang_w,
    sems,
    flat,
    bank,
    front,
    wide,
    joined,
    merged,
    pre,
    attended,
    total,
    first,
    second,
):
    wb = 512
    eb, tb, pb = 40, 20, 20
    nb = 256
    copies = [
        pltpu.make_async_copy(source, target, sems.at[i])
        for i, (source, target) in enumerate(
            [
                (front_h, front_w),
                (expand_h, expand_w),
                (pair_h, pair_w),
                (merge_h, merge_w),
                (squeeze_h, squeeze_w),
                (excite_h, excite_w),
                (attend_h, attend_w),
                (score_h, score_w),
                (embed_h, embed_w),
                (lang_h, lang_w),
            ]
        )
    ]
    copies[0].start()

    for s in range(SLOTS):
        flat[pl.ds(s, ROWS, stride=SLOTS), :] = recv_ref[s].astype(F32)
    header = flat[FLAT * SLOTS : (FLAT + 1) * SLOTS]
    bank[0] = jnp.zeros((BLOCKS, SLOTS, LANES), BF16)
    bank[NSUPER + 1] = jnp.zeros((BLOCKS, SLOTS, LANES), BF16)
    bank[1 : NSUPER + 1] = (
        flat[: FLAT * SLOTS].astype(BF16).reshape(NSUPER, BLOCKS, SLOTS, LANES)
    )

    copies[0].wait()
    for copy in copies[1:]:
        copy.start()

    nk = nb // LANES

    def front_cols(n, carry):
        cols = pl.ds(pl.multiple_of(n * wb, wb), wb)
        blocks = [n * (wb // LANES) + k for k in range(wb // LANES)]
        for j in range(SUPER):
            start = MELS * (j - 2)
            block, offset = start // LANES, start % LANES
            window = jnp.concatenate(
                [
                    bank[1 + t // BLOCKS : 1 + t // BLOCKS + NSUPER, t % BLOCKS]
                    for t in range(block, block + 4)
                ],
                axis=2,
            ).reshape(NSUPER * SLOTS, 4 * LANES)
            top = PAD_TOP - offset
            out = dot(window, front_w[top : top + 4 * LANES, cols])
            if j == 0:
                sample = jnp.maximum(out, 0.0).reshape(NSUPER, SLOTS, wb)
                first[:, cols] = jnp.sum(sample, axis=0) * (1.0 / NSUPER)
            out = jnp.maximum(out, 0.0).astype(BF16).reshape(NSUPER, SLOTS, wb)
            for i, k in enumerate(blocks):
                front[:, j, k] = out[:, :, i * LANES : (i + 1) * LANES]
        return carry

    lax.fori_loop(0, CH // wb, front_cols, 0)

    nf = CH // LANES
    frames = front.reshape(FRAMES, nf, SLOTS, LANES)

    copies[1].wait()
    edge = jnp.zeros((2, nf, SLOTS, LANES), BF16)
    wide[0:2] = edge
    wide[FRAMES + 2 : FRAMES + 4] = edge

    def expand_rows(f0):
        rows = get(frames, slice(f0, f0 + eb), range(nf)).reshape(eb * SLOTS, CH)
        for n in range(CH // nb):
            cols = slice(n * nb, (n + 1) * nb)
            out = jnp.maximum(dot(rows, expand_w[:, cols]), 0.0).astype(BF16)
            out = out.reshape(eb, SLOTS, nb)
            put(wide, slice(f0 + 2, f0 + 2 + eb), range(n * nk, (n + 1) * nk), out)
            if n == 0:
                joined[slice(f0, f0 + eb), 0] = out[:, :, :BR]

    for f0 in range(0, FRAMES, eb):
        expand_rows(f0)

    copies[2].wait()
    nq = FRAMES // 4
    quads = wide.reshape(nq + 1, 4, nf, SLOTS, LANES)
    outs = joined.reshape(nq, 4, nf, SLOTS, LANES)
    for i in range(1, SCALE):
        cut = nq // 2 + SCALE // 2 - i
        for lo, hi in ((0, cut), (cut, nq)):
            n = hi - lo
            rows = jnp.concatenate(
                [
                    jnp.concatenate(
                        [
                            quads[lo:hi, p, i],
                            quads[lo:hi, p + 2, i],
                            quads[lo + 1 : hi + 1, p, i],
                            quads[lo + 1 : hi + 1, p + 2, i],
                        ],
                        axis=2,
                    )
                    for p in range(2)
                ],
                axis=0,
            ).reshape(2 * n * SLOTS, 4 * BR)
            out = jnp.maximum(dot(rows, pair_w[i - 1]), 0.0).astype(BF16)
            out = out.reshape(2, n, SLOTS, 2 * BR)
            for p in range(2):
                early, late = out[p, :, :, :BR], out[p, :, :, BR:]
                outs[lo:hi, p, i] = early
                outs[lo:hi, p + 2, i] = late
                if i < SCALE - 1:
                    quads[lo:hi, p + 2, i + 1] = quads[lo:hi, p + 2, i + 1] + early
                    quads[lo + 1 : hi + 1, p, i + 1] = quads[lo + 1 : hi + 1, p, i + 1] + late

    copies[3].wait()
    total[...] = jnp.zeros_like(total)

    def merge_rows(f0):
        rows = get(joined, slice(f0, f0 + eb), range(nf)).reshape(eb * SLOTS, CH)
        for n in range(CH // nb):
            cols = slice(n * nb, (n + 1) * nb)
            out = jnp.maximum(dot(rows, merge_w[:, cols]), 0.0).reshape(eb, SLOTS, nb)
            put(merged, slice(f0, f0 + eb), range(n * nk, (n + 1) * nk), out.astype(BF16))
            total[:, cols] += jnp.sum(out, axis=0)

    for f0 in range(0, FRAMES, eb):
        merge_rows(f0)

    for k in range(4, 10):
        copies[k].wait()
    squeezed = total[...] * (1.0 / FRAMES)
    hidden = jnp.maximum(exact_dot(squeezed, squeeze_w[...]), 0.0)
    excited = jax.nn.sigmoid(exact_dot(hidden, excite_w[...]))
    gate = excited.astype(BF16)

    shift = (first[...] + squeezed * excited).astype(BF16)
    first[...] = jnp.zeros_like(first)
    second[...] = jnp.zeros_like(second)

    def trunk_rows(f0):
        acc = jnp.zeros((tb * SLOTS, ATT), F32)
        for n in range(CH // nb):
            cols = slice(n * nb, (n + 1) * nb)
            blocks = range(n * nk, (n + 1) * nk)
            out = get(frames, slice(f0, f0 + tb), blocks) + (
                get(merged, slice(f0, f0 + tb), blocks) * gate[:, cols][None]
            )
            put(frames, slice(f0, f0 + tb), blocks, out)
            off = out - shift[:, cols][None]
            first[:, cols] += slot_sums(fours(off))
            second[:, cols] += slot_sums(fours(off * off))
            acc = acc + dot(out.reshape(tb * SLOTS, nb), attend_w[cols, :])
        pre[slice(f0, f0 + tb)] = acc.reshape(tb, SLOTS, ATT)

    for f0 in range(0, FRAMES, tb):
        trunk_rows(f0)

    drift = first[...] * (1.0 / FRAMES)
    center = shift.astype(F32) + drift
    variance = jnp.maximum(second[...] * (1.0 / FRAMES) - drift * drift, 0.0)
    spread = jnp.sqrt(variance + EPS_STAT)
    context = exact_dot(center, attend_w[CH : 2 * CH]) + exact_dot(spread, attend_w[2 * CH :])
    attended[...] = (jnp.tanh(pre[...] + context[None]) * LOG2E).astype(BF16)

    first[...] = center
    second[...] = 1.0 / spread

    for n in range(CH // nb):
        cols = slice(n * nb, (n + 1) * nb)
        blocks = range(n * nk, (n + 1) * nk)
        middle = first[:, cols].astype(BF16)
        scale = second[:, cols].astype(BF16)
        parts = []
        for f0 in range(0, FRAMES, pb):
            rows = attended[f0 : f0 + pb].reshape(pb * SLOTS, ATT)
            energy = dot(rows, score_w[:, cols]).reshape(pb, SLOTS, nb)
            weight = jnp.exp2(energy).astype(BF16)
            z = (get(frames, slice(f0, f0 + pb), blocks) - middle[None]) * scale[None]
            wz = weight * z
            parts.append((fours(weight), fours(wz), fours(wz * z)))
        s0, s1, s2 = (slot_sums(jnp.concatenate(part, axis=0)) for part in zip(*parts))
        m1 = s1 / s0
        m2 = jnp.maximum(s2 / s0 - m1 * m1, 0.0)
        dev = 1.0 / scale.astype(F32)
        first[:, cols] = middle.astype(F32) + m1 * dev
        second[:, cols] = jnp.sqrt(m2 * dev * dev + EPS_STAT)
    pooled = jnp.concatenate([first[...], second[...]], axis=1).astype(BF16)
    embedding = dot(pooled, embed_w[...])
    logits = dot(embedding.astype(BF16), lang_w[...])
    mean_square = jnp.mean(jnp.square(embedding), axis=1, keepdims=True)
    normed = (embedding * lax.rsqrt(mean_square + EPS_NORM)).astype(BF16).astype(F32)
    high = logits.astype(BF16).astype(F32)
    fill = jnp.zeros((SLOTS, LANES - LANGS), F32)
    parts = [
        normed[:, :LANES],
        jnp.concatenate([normed[:, LANES:], header[:, : 2 * LANES - EMB]], axis=1),
        jnp.concatenate([high, fill], axis=1),
        jnp.concatenate([logits - high, fill], axis=1),
    ]
    for k, part in enumerate(parts):
        for m in range(8):
            flat[pl.ds(4 * m + k, SLOTS, stride=32), :] = part
    out_ref[...] = flat[: SLOTS * 32].astype(BF16)


def family(recv, weights):
    vmem = pl.BlockSpec(memory_space=pltpu.VMEM)
    away = pl.BlockSpec(memory_space=pl.ANY)
    return pl.pallas_call(
        family_kernel,
        out_shape=jax.ShapeDtypeStruct((SLOTS * 8 * 4, LANES), BF16),
        in_specs=[vmem] + [away] * len(weights),
        out_specs=vmem,
        scratch_shapes=[pltpu.VMEM(w.shape, w.dtype) for w in weights]
        + [
            pltpu.SemaphoreType.DMA((len(weights),)),
            pltpu.VMEM((ROWS * SLOTS, LANES), F32),
            pltpu.VMEM((NSUPER + 2, BLOCKS, SLOTS, LANES), BF16),
            pltpu.VMEM((NSUPER, SUPER, CH // LANES, SLOTS, LANES), BF16),
            pltpu.VMEM((FRAMES + 4, CH // LANES, SLOTS, LANES), BF16),
            pltpu.VMEM((FRAMES, CH // LANES, SLOTS, LANES), BF16),
            pltpu.VMEM((FRAMES, CH // LANES, SLOTS, LANES), BF16),
            pltpu.VMEM((FRAMES, SLOTS, ATT), F32),
            pltpu.VMEM((FRAMES, SLOTS, ATT), BF16),
            pltpu.VMEM((SLOTS, CH), F32),
            pltpu.VMEM((SLOTS, CH), F32),
            pltpu.VMEM((SLOTS, CH), F32),
        ],
        compiler_params=pltpu.CompilerParams(vmem_limit_bytes=52 << 20),
        cost_estimate=pl.CostEstimate(
            flops=20_000_000_000, bytes_accessed=10_000_000, transcendentals=4_000_000
        ),
        name="family",
    )(recv, *weights)


def home_kernel(mem_ref, recv_ref, logits_ref, sim_ref, flat, held):
    rows = recv_ref.shape[0] // 4
    flat[...] = recv_ref[...].astype(F32)
    parts = [flat[pl.ds(k, rows, stride=4), :] for k in range(4)]
    mark = parts[1][:, LANES - 1 :]
    row = lax.broadcasted_iota(jnp.int32, (rows, LANES), 0)
    lane = lax.broadcasted_iota(jnp.int32, (rows, LANES), 1)
    place = lax.rem(row, 8) * STORE + mark.astype(jnp.int32) - 1
    pick = jnp.where((mark > 0.5) & (place == lane), 1.0, 0.0).astype(BF16)
    held[...] = lax.dot_general(
        pick,
        jnp.concatenate(parts, axis=1).astype(BF16),
        (((0,), (0,)), ((), ())),
        preferred_element_type=F32,
    )
    own = held[pl.ds(pl.multiple_of(mem_ref[0] * STORE, STORE), STORE)]
    logits = own[:, 2 * LANES : 3 * LANES] + own[:, 3 * LANES :]
    logits_ref[0] = logits[:, :LANGS]
    sim = lax.dot_general(
        own[:, :EMB].astype(BF16),
        held[: 8 * STORE, :EMB].astype(BF16),
        (((1,), (1,)), ((), ())),
        preferred_element_type=F32,
    )
    sim_ref[0] = sim / EMB


def home(member, recv):
    vmem = pl.BlockSpec(memory_space=pltpu.VMEM)
    return pl.pallas_call(
        home_kernel,
        out_shape=(
            jax.ShapeDtypeStruct((1, STORE, LANGS), F32),
            jax.ShapeDtypeStruct((1, STORE, 8 * STORE), F32),
        ),
        in_specs=[pl.BlockSpec(memory_space=pltpu.SMEM), vmem],
        out_specs=(vmem, vmem),
        scratch_shapes=[
            pltpu.VMEM(recv.shape, F32),
            pltpu.VMEM((LANES, 4 * LANES), F32),
        ],
        compiler_params=pltpu.CompilerParams(vmem_limit_bytes=16 << 20),
        name="home",
    )(member, recv)


def prepare(initial_conv_weight, branch_weight):
    tall = jnp.pad(initial_conv_weight, ((PAD_TOP, PAD_TOP), (0, 0)))
    early = jnp.pad(branch_weight, ((0, 0), (0, BR), (0, 0)))
    late = jnp.pad(branch_weight, ((0, 0), (BR, 0), (0, 0)))
    return tall, jnp.concatenate([early, late], axis=2)


def shards(
    filterbank,
    destination,
    initial_conv_weight,
    expand_weight,
    branch_weight,
    merge_weight,
    squeeze_weight,
    excite_weight,
    attend_weight,
    score_weight,
    embed_weight,
    language_weight,
):
    bank = filterbank.reshape(STORE, FLAT, LANES).transpose(1, 0, 2)
    bank = bank.reshape(FLAT * STORE, LANES)
    outbound = pack(bank, destination.reshape(STORE))
    arrived = lax.all_to_all(outbound, "grp", split_axis=0, concat_axis=0, tiled=True)
    tall, pairs = prepare(initial_conv_weight, branch_weight)
    scored = family(
        arrived,
        (
            tall,
            expand_weight,
            pairs,
            merge_weight,
            squeeze_weight,
            excite_weight,
            attend_weight[0],
            score_weight[0],
            embed_weight[0],
            language_weight[0],
        ),
    )
    back = lax.all_to_all(
        scored.reshape(SLOTS * 8, 4, LANES),
        ("grp", "mem"),
        split_axis=0,
        concat_axis=0,
        tiled=True,
    )
    member = lax.axis_index("mem").astype(jnp.int32).reshape(1)
    return home(member, back.reshape(SLOTS * 8 * 4, LANES))


def solution(mesh):
    return jax.shard_map(
        shards,
        mesh=mesh,
        in_specs=(
            P("grp", "mem", None, None),
            P("grp", "mem"),
            P(),
            P(),
            P(),
            P(),
            P(),
            P(),
            P("grp", None, None),
            P("grp", None, None),
            P("grp", None, None),
            P("grp", None, None),
        ),
        out_specs=(P("grp", "mem", None), P("grp", "mem", None)),
        check_vma=False,
    )
```

```python
import functools

import jax
import jax.numpy as jnp
from jax import lax
from jax.experimental import pallas as pl
from jax.experimental.pallas import tpu as pltpu
from jax.sharding import PartitionSpec as P

MELS = 80
CH = 1024
BR = 128
SCALE = 8
ATT = 128
EMB = 192
LANGS = 107
FRAMES = 200
STORE = 8
SLOTS = 16
LANES = 128

FLAT = FRAMES * MELS // LANES
ROWS = 128

SUPER = 8
NSUPER = FRAMES // SUPER
WIDE = SUPER * MELS
BLOCKS = WIDE // LANES
TAPS = 5 * MELS
PAD_TOP = 112

EPS_STAT = 1e-05
EPS_NORM = 1e-06

LOG2E = 1.4426950408889634

F32 = jnp.float32
BF16 = jnp.bfloat16


def dot(a, b):
    return jnp.dot(a, b, preferred_element_type=F32)


def exact_dot(a, b):
    rows = a.shape[0]
    high = a.astype(BF16)
    rest = a - high.astype(F32)
    mid = rest.astype(BF16)
    low = (rest - mid.astype(F32)).astype(BF16)
    out = dot(jnp.concatenate([high, mid, low], axis=0), b)
    return out[:rows] + (out[rows : 2 * rows] + out[2 * rows :])


def pack_kernel(dest_ref, bank_ref, out_ref, row_ref):
    out_ref[...] = jnp.zeros_like(out_ref)
    for s in range(STORE):
        row_ref[:FLAT] = bank_ref[pl.ds(s, FLAT, stride=STORE), :]
        row_ref[FLAT:] = jnp.full((ROWS - FLAT, LANES), s + 1, F32)
        out_ref[dest_ref[s]] = row_ref[...].astype(BF16)


def pack(bank, dest):
    return pl.pallas_call(
        pack_kernel,
        out_shape=jax.ShapeDtypeStruct((SLOTS, ROWS, LANES), BF16),
        in_specs=[
            pl.BlockSpec(memory_space=pltpu.SMEM),
            pl.BlockSpec(memory_space=pltpu.VMEM),
        ],
        out_specs=pl.BlockSpec(memory_space=pltpu.VMEM),
        scratch_shapes=[pltpu.VMEM((ROWS, LANES), F32)],
        name="pack",
    )(dest, bank)


def slot_sums(values):
    frames, slots, columns = values.shape
    row = lax.broadcasted_iota(jnp.int32, (slots, frames * slots), 0)
    column = lax.broadcasted_iota(jnp.int32, (slots, frames * slots), 1)
    same = jnp.where(lax.rem(column, slots) == row, 1.0, 0.0).astype(BF16)
    return dot(same, values.reshape(frames * slots, columns))


def fours(values):
    frames, slots, columns = values.shape
    split = values.reshape(frames // 4, 4, slots, columns)
    return (split[:, 0] + split[:, 1]) + (split[:, 2] + split[:, 3])


def get(ref, frames, blocks):
    return jnp.concatenate([ref[frames, k] for k in blocks], axis=-1)


def put(ref, frames, blocks, values):
    for i, k in enumerate(blocks):
        ref[frames, k] = values[..., i * LANES : (i + 1) * LANES]


def family_kernel(
    recv_ref,
    front_h,
    expand_h,
    pair_h,
    merge_h,
    squeeze_h,
    excite_h,
    attend_h,
    score_h,
    embed_h,
    lang_h,
    out_ref,
    front_w,
    expand_w,
    pair_w,
    merge_w,
    squeeze_w,
    excite_w,
    attend_w,
    score_w,
    embed_w,
    lang_w,
    sems,
    flat,
    bank,
    front,
    wide,
    joined,
    merged,
    pre,
    attended,
    total,
    first,
    second,
):
    wb = 512
    eb, tb, pb = 40, 20, 20
    nb = 256
    copies = [
        pltpu.make_async_copy(source, target, sems.at[i])
        for i, (source, target) in enumerate(
            [
                (front_h, front_w),
                (expand_h, expand_w),
                (pair_h, pair_w),
                (merge_h, merge_w),
                (squeeze_h, squeeze_w),
                (excite_h, excite_w),
                (attend_h, attend_w),
                (score_h, score_w),
                (embed_h, embed_w),
                (lang_h, lang_w),
            ]
        )
    ]
    copies[0].start()

    for s in range(SLOTS):
        flat[pl.ds(s, ROWS, stride=SLOTS), :] = recv_ref[s].astype(F32)
    header = flat[FLAT * SLOTS : (FLAT + 1) * SLOTS]
    bank[0] = jnp.zeros((BLOCKS, SLOTS, LANES), BF16)
    bank[NSUPER + 1] = jnp.zeros((BLOCKS, SLOTS, LANES), BF16)
    bank[1 : NSUPER + 1] = (
        flat[: FLAT * SLOTS].astype(BF16).reshape(NSUPER, BLOCKS, SLOTS, LANES)
    )

    copies[0].wait()
    for copy in copies[1:]:
        copy.start()

    nk = nb // LANES

    def front_cols(n, carry):
        cols = pl.ds(pl.multiple_of(n * wb, wb), wb)
        blocks = [n * (wb // LANES) + k for k in range(wb // LANES)]
        for j in range(SUPER):
            start = MELS * (j - 2)
            block, offset = start // LANES, start % LANES
            window = jnp.concatenate(
                [
                    bank[1 + t // BLOCKS : 1 + t // BLOCKS + NSUPER, t % BLOCKS]
                    for t in range(block, block + 4)
                ],
                axis=2,
            ).reshape(NSUPER * SLOTS, 4 * LANES)
            top = PAD_TOP - offset
            out = dot(window, front_w[top : top + 4 * LANES, cols])
            if j == 0:
                sample = jnp.maximum(out, 0.0).reshape(NSUPER, SLOTS, wb)
                first[:, cols] = jnp.sum(sample, axis=0) * (1.0 / NSUPER)
            out = jnp.maximum(out, 0.0).astype(BF16).reshape(NSUPER, SLOTS, wb)
            for i, k in enumerate(blocks):
                front[:, j, k] = out[:, :, i * LANES : (i + 1) * LANES]
        return carry

    lax.fori_loop(0, CH // wb, front_cols, 0)

    nf = CH // LANES
    frames = front.reshape(FRAMES, nf, SLOTS, LANES)

    copies[1].wait()
    edge = jnp.zeros((2, nf, SLOTS, LANES), BF16)
    wide[0:2] = edge
    wide[FRAMES + 2 : FRAMES + 4] = edge

    def expand_rows(f0):
        rows = get(frames, slice(f0, f0 + eb), range(nf)).reshape(eb * SLOTS, CH)
        for n in range(CH // nb):
            cols = slice(n * nb, (n + 1) * nb)
            out = jnp.maximum(dot(rows, expand_w[:, cols]), 0.0).astype(BF16)
            out = out.reshape(eb, SLOTS, nb)
            put(wide, slice(f0 + 2, f0 + 2 + eb), range(n * nk, (n + 1) * nk), out)
            if n == 0:
                joined[slice(f0, f0 + eb), 0] = out[:, :, :BR]

    for f0 in range(0, FRAMES, eb):
        expand_rows(f0)

    copies[2].wait()
    nq = FRAMES // 4
    quads = wide.reshape(nq + 1, 4, nf, SLOTS, LANES)
    outs = joined.reshape(nq, 4, nf, SLOTS, LANES)
    for i in range(1, SCALE):
        cut = nq // 2 + SCALE // 2 - i
        for lo, hi in ((0, cut), (cut, nq)):
            n = hi - lo
            rows = jnp.concatenate(
                [
                    jnp.concatenate(
                        [
                            quads[lo:hi, p, i],
                            quads[lo:hi, p + 2, i],
                            quads[lo + 1 : hi + 1, p, i],
                            quads[lo + 1 : hi + 1, p + 2, i],
                        ],
                        axis=2,
                    )
                    for p in range(2)
                ],
                axis=0,
            ).reshape(2 * n * SLOTS, 4 * BR)
            out = jnp.maximum(dot(rows, pair_w[i - 1]), 0.0).astype(BF16)
            out = out.reshape(2, n, SLOTS, 2 * BR)
            for p in range(2):
                early, late = out[p, :, :, :BR], out[p, :, :, BR:]
                outs[lo:hi, p, i] = early
                outs[lo:hi, p + 2, i] = late
                if i < SCALE - 1:
                    quads[lo:hi, p + 2, i + 1] = quads[lo:hi, p + 2, i + 1] + early
                    quads[lo + 1 : hi + 1, p, i + 1] = quads[lo + 1 : hi + 1, p, i + 1] + late

    copies[3].wait()
    total[...] = jnp.zeros_like(total)

    def merge_rows(f0):
        rows = get(joined, slice(f0, f0 + eb), range(nf)).reshape(eb * SLOTS, CH)
        for n in range(CH // nb):
            cols = slice(n * nb, (n + 1) * nb)
            out = jnp.maximum(dot(rows, merge_w[:, cols]), 0.0).reshape(eb, SLOTS, nb)
            put(merged, slice(f0, f0 + eb), range(n * nk, (n + 1) * nk), out.astype(BF16))
            total[:, cols] += jnp.sum(out, axis=0)

    for f0 in range(0, FRAMES, eb):
        merge_rows(f0)

    for k in range(4, 10):
        copies[k].wait()
    squeezed = total[...] * (1.0 / FRAMES)
    hidden = jnp.maximum(exact_dot(squeezed, squeeze_w[...]), 0.0)
    excited = jax.nn.sigmoid(exact_dot(hidden, excite_w[...]))
    gate = excited.astype(BF16)

    shift = (first[...] + squeezed * excited).astype(BF16)
    first[...] = jnp.zeros_like(first)
    second[...] = jnp.zeros_like(second)

    def trunk_rows(f0):
        acc = jnp.zeros((tb * SLOTS, ATT), F32)
        for n in range(CH // nb):
            cols = slice(n * nb, (n + 1) * nb)
            blocks = range(n * nk, (n + 1) * nk)
            out = get(frames, slice(f0, f0 + tb), blocks) + (
                get(merged, slice(f0, f0 + tb), blocks) * gate[:, cols][None]
            )
            put(frames, slice(f0, f0 + tb), blocks, out)
            off = out - shift[:, cols][None]
            first[:, cols] += slot_sums(fours(off))
            second[:, cols] += slot_sums(fours(off * off))
            acc = acc + dot(out.reshape(tb * SLOTS, nb), attend_w[cols, :])
        pre[slice(f0, f0 + tb)] = acc.reshape(tb, SLOTS, ATT)

    for f0 in range(0, FRAMES, tb):
        trunk_rows(f0)

    drift = first[...] * (1.0 / FRAMES)
    center = shift.astype(F32) + drift
    variance = jnp.maximum(second[...] * (1.0 / FRAMES) - drift * drift, 0.0)
    spread = jnp.sqrt(variance + EPS_STAT)
    context = exact_dot(center, attend_w[CH : 2 * CH]) + exact_dot(spread, attend_w[2 * CH :])
    attended[...] = (jnp.tanh(pre[...] + context[None]) * LOG2E).astype(BF16)

    first[...] = center
    second[...] = 1.0 / spread

    for n in range(CH // nb):
        cols = slice(n * nb, (n + 1) * nb)
        blocks = range(n * nk, (n + 1) * nk)
        middle = first[:, cols].astype(BF16)
        scale = second[:, cols].astype(BF16)
        parts = []
        for f0 in range(0, FRAMES, pb):
            rows = attended[f0 : f0 + pb].reshape(pb * SLOTS, ATT)
            energy = dot(rows, score_w[:, cols]).reshape(pb, SLOTS, nb)
            weight = jnp.exp2(energy).astype(BF16)
            z = (get(frames, slice(f0, f0 + pb), blocks) - middle[None]) * scale[None]
            put(joined, slice(f0, f0 + pb), blocks, weight)
            parts.append((fours(weight), fours(weight * z)))
        s0, s1 = (slot_sums(jnp.concatenate(part, axis=0)) for part in zip(*parts))
        dev = 1.0 / scale.astype(F32)
        middle = (middle.astype(F32) + s1 / s0 * dev).astype(BF16)
        parts = []
        for f0 in range(0, FRAMES, pb):
            z = (get(frames, slice(f0, f0 + pb), blocks) - middle[None]) * scale[None]
            wz = get(joined, slice(f0, f0 + pb), blocks) * z
            parts.append((fours(wz), fours(wz * z)))
        s1, s2 = (slot_sums(jnp.concatenate(part, axis=0)) for part in zip(*parts))
        m1 = s1 / s0
        m2 = jnp.maximum(s2 / s0 - m1 * m1, 0.0)
        first[:, cols] = middle.astype(F32) + m1 * dev
        second[:, cols] = jnp.sqrt(m2 * dev * dev + EPS_STAT)
    pooled = jnp.concatenate([first[...], second[...]], axis=1).astype(BF16)
    embedding = dot(pooled, embed_w[...])
    logits = dot(embedding.astype(BF16), lang_w[...])
    mean_square = jnp.mean(jnp.square(embedding), axis=1, keepdims=True)
    normed = (embedding * lax.rsqrt(mean_square + EPS_NORM)).astype(BF16).astype(F32)
    high = logits.astype(BF16).astype(F32)
    fill = jnp.zeros((SLOTS, LANES - LANGS), F32)
    parts = [
        normed[:, :LANES],
        jnp.concatenate([normed[:, LANES:], header[:, : 2 * LANES - EMB]], axis=1),
        jnp.concatenate([high, fill], axis=1),
        jnp.concatenate([logits - high, fill], axis=1),
    ]
    for k, part in enumerate(parts):
        for m in range(8):
            flat[pl.ds(4 * m + k, SLOTS, stride=32), :] = part
    out_ref[...] = flat[: SLOTS * 32].astype(BF16)


def family(recv, weights):
    vmem = pl.BlockSpec(memory_space=pltpu.VMEM)
    away = pl.BlockSpec(memory_space=pl.ANY)
    return pl.pallas_call(
        family_kernel,
        out_shape=jax.ShapeDtypeStruct((SLOTS * 8 * 4, LANES), BF16),
        in_specs=[vmem] + [away] * len(weights),
        out_specs=vmem,
        scratch_shapes=[pltpu.VMEM(w.shape, w.dtype) for w in weights]
        + [
            pltpu.SemaphoreType.DMA((len(weights),)),
            pltpu.VMEM((ROWS * SLOTS, LANES), F32),
            pltpu.VMEM((NSUPER + 2, BLOCKS, SLOTS, LANES), BF16),
            pltpu.VMEM((NSUPER, SUPER, CH // LANES, SLOTS, LANES), BF16),
            pltpu.VMEM((FRAMES + 4, CH // LANES, SLOTS, LANES), BF16),
            pltpu.VMEM((FRAMES, CH // LANES, SLOTS, LANES), BF16),
            pltpu.VMEM((FRAMES, CH // LANES, SLOTS, LANES), BF16),
            pltpu.VMEM((FRAMES, SLOTS, ATT), F32),
            pltpu.VMEM((FRAMES, SLOTS, ATT), BF16),
            pltpu.VMEM((SLOTS, CH), F32),
            pltpu.VMEM((SLOTS, CH), F32),
            pltpu.VMEM((SLOTS, CH), F32),
        ],
        compiler_params=pltpu.CompilerParams(vmem_limit_bytes=52 << 20),
        cost_estimate=pl.CostEstimate(
            flops=20_000_000_000, bytes_accessed=10_000_000, transcendentals=4_000_000
        ),
        name="family",
    )(recv, *weights)


def home_kernel(mem_ref, recv_ref, logits_ref, sim_ref, flat, held):
    rows = recv_ref.shape[0] // 4
    flat[...] = recv_ref[...].astype(F32)
    parts = [flat[pl.ds(k, rows, stride=4), :] for k in range(4)]
    mark = parts[1][:, LANES - 1 :]
    row = lax.broadcasted_iota(jnp.int32, (rows, LANES), 0)
    lane = lax.broadcasted_iota(jnp.int32, (rows, LANES), 1)
    place = lax.rem(row, 8) * STORE + mark.astype(jnp.int32) - 1
    pick = jnp.where((mark > 0.5) & (place == lane), 1.0, 0.0).astype(BF16)
    held[...] = lax.dot_general(
        pick,
        jnp.concatenate(parts, axis=1).astype(BF16),
        (((0,), (0,)), ((), ())),
        preferred_element_type=F32,
    )
    own = held[pl.ds(pl.multiple_of(mem_ref[0] * STORE, STORE), STORE)]
    logits = own[:, 2 * LANES : 3 * LANES] + own[:, 3 * LANES :]
    logits_ref[0] = logits[:, :LANGS]
    sim = lax.dot_general(
        own[:, :EMB].astype(BF16),
        held[: 8 * STORE, :EMB].astype(BF16),
        (((1,), (1,)), ((), ())),
        preferred_element_type=F32,
    )
    sim_ref[0] = sim / EMB


def home(member, recv):
    vmem = pl.BlockSpec(memory_space=pltpu.VMEM)
    return pl.pallas_call(
        home_kernel,
        out_shape=(
            jax.ShapeDtypeStruct((1, STORE, LANGS), F32),
            jax.ShapeDtypeStruct((1, STORE, 8 * STORE), F32),
        ),
        in_specs=[pl.BlockSpec(memory_space=pltpu.SMEM), vmem],
        out_specs=(vmem, vmem),
        scratch_shapes=[
            pltpu.VMEM(recv.shape, F32),
            pltpu.VMEM((LANES, 4 * LANES), F32),
        ],
        compiler_params=pltpu.CompilerParams(vmem_limit_bytes=16 << 20),
        name="home",
    )(member, recv)


def prepare(initial_conv_weight, branch_weight):
    tall = jnp.pad(initial_conv_weight, ((PAD_TOP, PAD_TOP), (0, 0)))
    early = jnp.pad(branch_weight, ((0, 0), (0, BR), (0, 0)))
    late = jnp.pad(branch_weight, ((0, 0), (BR, 0), (0, 0)))
    return tall, jnp.concatenate([early, late], axis=2)


def shards(
    filterbank,
    destination,
    initial_conv_weight,
    expand_weight,
    branch_weight,
    merge_weight,
    squeeze_weight,
    excite_weight,
    attend_weight,
    score_weight,
    embed_weight,
    language_weight,
):
    bank = filterbank.reshape(STORE, FLAT, LANES).transpose(1, 0, 2)
    bank = bank.reshape(FLAT * STORE, LANES)
    outbound = pack(bank, destination.reshape(STORE))
    arrived = lax.all_to_all(outbound, "grp", split_axis=0, concat_axis=0, tiled=True)
    tall, pairs = prepare(initial_conv_weight, branch_weight)
    scored = family(
        arrived,
        (
            tall,
            expand_weight,
            pairs,
            merge_weight,
            squeeze_weight,
            excite_weight,
            attend_weight[0],
            score_weight[0],
            embed_weight[0],
            language_weight[0],
        ),
    )
    back = lax.all_to_all(
        scored.reshape(SLOTS * 8, 4, LANES),
        ("grp", "mem"),
        split_axis=0,
        concat_axis=0,
        tiled=True,
    )
    member = lax.axis_index("mem").astype(jnp.int32).reshape(1)
    return home(member, back.reshape(SLOTS * 8 * 4, LANES))


def solution(mesh):
    return jax.shard_map(
        shards,
        mesh=mesh,
        in_specs=(
            P("grp", "mem", None, None),
            P("grp", "mem"),
            P(),
            P(),
            P(),
            P(),
            P(),
            P(),
            P("grp", None, None),
            P("grp", None, None),
            P("grp", None, None),
            P("grp", None, None),
        ),
        out_specs=(P("grp", "mem", None), P("grp", "mem", None)),
        check_vma=False,
    )
```

```python
import functools

import jax
import jax.numpy as jnp
from jax import lax
from jax.experimental import pallas as pl
from jax.experimental.pallas import tpu as pltpu
from jax.sharding import PartitionSpec as P

MELS = 80
CH = 1024
BR = 128
SCALE = 8
ATT = 128
EMB = 192
LANGS = 107
FRAMES = 200
STORE = 8
SLOTS = 16
LANES = 128

FLAT = FRAMES * MELS // LANES
ROWS = 128

SUPER = 8
NSUPER = FRAMES // SUPER
WIDE = SUPER * MELS
BLOCKS = WIDE // LANES
TAPS = 5 * MELS
PAD_TOP = 112

EPS_STAT = 1e-05
EPS_NORM = 1e-06

LOG2E = 1.4426950408889634

F32 = jnp.float32
BF16 = jnp.bfloat16


def dot(a, b):
    return jnp.dot(a, b, preferred_element_type=F32)


def exact_dot(a, b):
    rows = a.shape[0]
    high = a.astype(BF16)
    rest = a - high.astype(F32)
    mid = rest.astype(BF16)
    low = (rest - mid.astype(F32)).astype(BF16)
    out = dot(jnp.concatenate([high, mid, low], axis=0), b)
    return out[:rows] + (out[rows : 2 * rows] + out[2 * rows :])


def pack_kernel(dest_ref, bank_ref, out_ref, row_ref):
    out_ref[...] = jnp.zeros_like(out_ref)
    for s in range(STORE):
        row_ref[:FLAT] = bank_ref[pl.ds(s, FLAT, stride=STORE), :]
        row_ref[FLAT:] = jnp.full((ROWS - FLAT, LANES), s + 1, F32)
        out_ref[dest_ref[s]] = row_ref[...].astype(BF16)


def pack(bank, dest):
    return pl.pallas_call(
        pack_kernel,
        out_shape=jax.ShapeDtypeStruct((SLOTS, ROWS, LANES), BF16),
        in_specs=[
            pl.BlockSpec(memory_space=pltpu.SMEM),
            pl.BlockSpec(memory_space=pltpu.VMEM),
        ],
        out_specs=pl.BlockSpec(memory_space=pltpu.VMEM),
        scratch_shapes=[pltpu.VMEM((ROWS, LANES), F32)],
        name="pack",
    )(dest, bank)


def slot_sums(values):
    frames, slots, columns = values.shape
    row = lax.broadcasted_iota(jnp.int32, (slots, frames * slots), 0)
    column = lax.broadcasted_iota(jnp.int32, (slots, frames * slots), 1)
    same = jnp.where(lax.rem(column, slots) == row, 1.0, 0.0).astype(BF16)
    return dot(same, values.reshape(frames * slots, columns))


def fours(values):
    frames, slots, columns = values.shape
    split = values.reshape(frames // 4, 4, slots, columns)
    return (split[:, 0] + split[:, 1]) + (split[:, 2] + split[:, 3])


def get(ref, frames, blocks):
    return jnp.concatenate([ref[frames, k] for k in blocks], axis=-1)


def put(ref, frames, blocks, values):
    for i, k in enumerate(blocks):
        ref[frames, k] = values[..., i * LANES : (i + 1) * LANES]


def family_kernel(
    recv_ref,
    front_h,
    expand_h,
    pair_h,
    merge_h,
    squeeze_h,
    excite_h,
    attend_h,
    score_h,
    embed_h,
    lang_h,
    out_ref,
    front_w,
    expand_w,
    pair_w,
    merge_w,
    squeeze_w,
    excite_w,
    attend_w,
    score_w,
    embed_w,
    lang_w,
    sems,
    flat,
    bank,
    front,
    wide,
    joined,
    merged,
    pre,
    attended,
    total,
    first,
    second,
):
    wb = 512
    eb, tb, pb = 40, 20, 20
    nb = 256
    copies = [
        pltpu.make_async_copy(source, target, sems.at[i])
        for i, (source, target) in enumerate(
            [
                (front_h, front_w),
                (expand_h, expand_w),
                (pair_h, pair_w),
                (merge_h, merge_w),
                (squeeze_h, squeeze_w),
                (excite_h, excite_w),
                (attend_h, attend_w),
                (score_h, score_w),
                (embed_h, embed_w),
                (lang_h, lang_w),
            ]
        )
    ]
    copies[0].start()

    for s in range(SLOTS):
        flat[pl.ds(s, ROWS, stride=SLOTS), :] = recv_ref[s].astype(F32)
    header = flat[FLAT * SLOTS : (FLAT + 1) * SLOTS]
    bank[0] = jnp.zeros((BLOCKS, SLOTS, LANES), BF16)
    bank[NSUPER + 1] = jnp.zeros((BLOCKS, SLOTS, LANES), BF16)
    bank[1 : NSUPER + 1] = (
        flat[: FLAT * SLOTS].astype(BF16).reshape(NSUPER, BLOCKS, SLOTS, LANES)
    )

    copies[0].wait()
    for copy in copies[1:]:
        copy.start()

    nk = nb // LANES

    def front_cols(n, carry):
        cols = pl.ds(pl.multiple_of(n * wb, wb), wb)
        blocks = [n * (wb // LANES) + k for k in range(wb // LANES)]
        for j in range(SUPER):
            start = MELS * (j - 2)
            block, offset = start // LANES, start % LANES
            window = jnp.concatenate(
                [
                    bank[1 + t // BLOCKS : 1 + t // BLOCKS + NSUPER, t % BLOCKS]
                    for t in range(block, block + 4)
                ],
                axis=2,
            ).reshape(NSUPER * SLOTS, 4 * LANES)
            top = PAD_TOP - offset
            out = dot(window, front_w[top : top + 4 * LANES, cols])
            if j == 0:
                sample = jnp.maximum(out, 0.0).reshape(NSUPER, SLOTS, wb)
                first[:, cols] = jnp.sum(sample, axis=0) * (1.0 / NSUPER)
            out = jnp.maximum(out, 0.0).astype(BF16).reshape(NSUPER, SLOTS, wb)
            for i, k in enumerate(blocks):
                front[:, j, k] = out[:, :, i * LANES : (i + 1) * LANES]
        return carry

    lax.fori_loop(0, CH // wb, front_cols, 0)

    nf = CH // LANES
    frames = front.reshape(FRAMES, nf, SLOTS, LANES)

    copies[1].wait()
    edge = jnp.zeros((2, nf, SLOTS, LANES), BF16)
    wide[0:2] = edge
    wide[FRAMES + 2 : FRAMES + 4] = edge

    def expand_rows(f0):
        rows = get(frames, slice(f0, f0 + eb), range(nf)).reshape(eb * SLOTS, CH)
        for n in range(CH // nb):
            cols = slice(n * nb, (n + 1) * nb)
            out = jnp.maximum(dot(rows, expand_w[:, cols]), 0.0).astype(BF16)
            out = out.reshape(eb, SLOTS, nb)
            put(wide, slice(f0 + 2, f0 + 2 + eb), range(n * nk, (n + 1) * nk), out)
            if n == 0:
                joined[slice(f0, f0 + eb), 0] = out[:, :, :BR]

    for f0 in range(0, FRAMES, eb):
        expand_rows(f0)

    copies[2].wait()
    nq = FRAMES // 4
    quads = wide.reshape(nq + 1, 4, nf, SLOTS, LANES)
    outs = joined.reshape(nq, 4, nf, SLOTS, LANES)
    for i in range(1, SCALE):
        cut = nq // 2 + SCALE // 2 - i
        for lo, hi in ((0, cut), (cut, nq)):
            n = hi - lo
            rows = jnp.concatenate(
                [
                    jnp.concatenate(
                        [
                            quads[lo:hi, p, i],
                            quads[lo:hi, p + 2, i],
                            quads[lo + 1 : hi + 1, p, i],
                            quads[lo + 1 : hi + 1, p + 2, i],
                        ],
                        axis=2,
                    )
                    for p in range(2)
                ],
                axis=0,
            ).reshape(2 * n * SLOTS, 4 * BR)
            out = jnp.maximum(dot(rows, pair_w[i - 1]), 0.0).astype(BF16)
            out = out.reshape(2, n, SLOTS, 2 * BR)
            for p in range(2):
                early, late = out[p, :, :, :BR], out[p, :, :, BR:]
                outs[lo:hi, p, i] = early
                outs[lo:hi, p + 2, i] = late
                if i < SCALE - 1:
                    quads[lo:hi, p + 2, i + 1] = quads[lo:hi, p + 2, i + 1] + early
                    quads[lo + 1 : hi + 1, p, i + 1] = quads[lo + 1 : hi + 1, p, i + 1] + late

    copies[3].wait()
    total[...] = jnp.zeros_like(total)

    def merge_rows(f0):
        rows = get(joined, slice(f0, f0 + eb), range(nf)).reshape(eb * SLOTS, CH)
        for n in range(CH // nb):
            cols = slice(n * nb, (n + 1) * nb)
            out = jnp.maximum(dot(rows, merge_w[:, cols]), 0.0).reshape(eb, SLOTS, nb)
            put(merged, slice(f0, f0 + eb), range(n * nk, (n + 1) * nk), out.astype(BF16))
            total[:, cols] += jnp.sum(out, axis=0)

    for f0 in range(0, FRAMES, eb):
        merge_rows(f0)

    for k in range(4, 10):
        copies[k].wait()
    squeezed = total[...] * (1.0 / FRAMES)
    hidden = jnp.maximum(exact_dot(squeezed, squeeze_w[...]), 0.0)
    excited = jax.nn.sigmoid(exact_dot(hidden, excite_w[...]))
    gate = excited.astype(BF16)

    shift = (first[...] + squeezed * excited).astype(BF16)
    first[...] = jnp.zeros_like(first)
    second[...] = jnp.zeros_like(second)

    def trunk_rows(f0):
        acc = jnp.zeros((tb * SLOTS, ATT), F32)
        for n in range(CH // nb):
            cols = slice(n * nb, (n + 1) * nb)
            blocks = range(n * nk, (n + 1) * nk)
            out = get(frames, slice(f0, f0 + tb), blocks) + (
                get(merged, slice(f0, f0 + tb), blocks) * gate[:, cols][None]
            )
            put(frames, slice(f0, f0 + tb), blocks, out)
            off = out - shift[:, cols][None]
            first[:, cols] += slot_sums(fours(off))
            second[:, cols] += slot_sums(fours(off * off))
            acc = acc + dot(out.reshape(tb * SLOTS, nb), attend_w[cols, :])
        pre[slice(f0, f0 + tb)] = acc.reshape(tb, SLOTS, ATT)

    for f0 in range(0, FRAMES, tb):
        trunk_rows(f0)

    drift = first[...] * (1.0 / FRAMES)
    center = shift.astype(F32) + drift
    variance = jnp.maximum(second[...] * (1.0 / FRAMES) - drift * drift, 0.0)
    spread = jnp.sqrt(variance + EPS_STAT)
    context = exact_dot(center, attend_w[CH : 2 * CH]) + exact_dot(spread, attend_w[2 * CH :])
    attended[...] = (jnp.tanh(pre[...] + context[None]) * LOG2E).astype(BF16)

    first[...] = center
    second[...] = 1.0 / spread

    for n in range(CH // nb):
        cols = slice(n * nb, (n + 1) * nb)
        blocks = range(n * nk, (n + 1) * nk)
        middle = first[:, cols].astype(BF16)
        scale = second[:, cols].astype(BF16)
        parts = []
        for f0 in range(0, FRAMES, pb):
            rows = attended[f0 : f0 + pb].reshape(pb * SLOTS, ATT)
            energy = dot(rows, score_w[:, cols]).reshape(pb, SLOTS, nb)
            weight = jnp.exp2(energy)
            z = (get(frames, slice(f0, f0 + pb), blocks) - middle[None]) * scale[None]
            z = z.astype(F32)
            wz = weight * z
            parts.append([jnp.sum(part, axis=0) for part in (weight, wz, wz * z)])
        s0, s1, s2 = (sum(part) for part in zip(*parts))
        m1 = s1 / s0
        m2 = jnp.maximum(s2 / s0 - m1 * m1, 0.0)
        dev = 1.0 / scale.astype(F32)
        first[:, cols] = middle.astype(F32) + m1 * dev
        second[:, cols] = jnp.sqrt(m2 * dev * dev + EPS_STAT)
    pooled = jnp.concatenate([first[...], second[...]], axis=1).astype(BF16)
    embedding = dot(pooled, embed_w[...])
    logits = dot(embedding.astype(BF16), lang_w[...])
    mean_square = jnp.mean(jnp.square(embedding), axis=1, keepdims=True)
    normed = (embedding * lax.rsqrt(mean_square + EPS_NORM)).astype(BF16).astype(F32)
    high = logits.astype(BF16).astype(F32)
    fill = jnp.zeros((SLOTS, LANES - LANGS), F32)
    parts = [
        normed[:, :LANES],
        jnp.concatenate([normed[:, LANES:], header[:, : 2 * LANES - EMB]], axis=1),
        jnp.concatenate([high, fill], axis=1),
        jnp.concatenate([logits - high, fill], axis=1),
    ]
    for k, part in enumerate(parts):
        for m in range(8):
            flat[pl.ds(4 * m + k, SLOTS, stride=32), :] = part
    out_ref[...] = flat[: SLOTS * 32].astype(BF16)


def family(recv, weights):
    vmem = pl.BlockSpec(memory_space=pltpu.VMEM)
    away = pl.BlockSpec(memory_space=pl.ANY)
    return pl.pallas_call(
        family_kernel,
        out_shape=jax.ShapeDtypeStruct((SLOTS * 8 * 4, LANES), BF16),
        in_specs=[vmem] + [away] * len(weights),
        out_specs=vmem,
        scratch_shapes=[pltpu.VMEM(w.shape, w.dtype) for w in weights]
        + [
            pltpu.SemaphoreType.DMA((len(weights),)),
            pltpu.VMEM((ROWS * SLOTS, LANES), F32),
            pltpu.VMEM((NSUPER + 2, BLOCKS, SLOTS, LANES), BF16),
            pltpu.VMEM((NSUPER, SUPER, CH // LANES, SLOTS, LANES), BF16),
            pltpu.VMEM((FRAMES + 4, CH // LANES, SLOTS, LANES), BF16),
            pltpu.VMEM((FRAMES, CH // LANES, SLOTS, LANES), BF16),
            pltpu.VMEM((FRAMES, CH // LANES, SLOTS, LANES), BF16),
            pltpu.VMEM((FRAMES, SLOTS, ATT), F32),
            pltpu.VMEM((FRAMES, SLOTS, ATT), BF16),
            pltpu.VMEM((SLOTS, CH), F32),
            pltpu.VMEM((SLOTS, CH), F32),
            pltpu.VMEM((SLOTS, CH), F32),
        ],
        compiler_params=pltpu.CompilerParams(vmem_limit_bytes=52 << 20),
        cost_estimate=pl.CostEstimate(
            flops=20_000_000_000, bytes_accessed=10_000_000, transcendentals=4_000_000
        ),
        name="family",
    )(recv, *weights)


def home_kernel(mem_ref, recv_ref, logits_ref, sim_ref, flat, held):
    rows = recv_ref.shape[0] // 4
    flat[...] = recv_ref[...].astype(F32)
    parts = [flat[pl.ds(k, rows, stride=4), :] for k in range(4)]
    mark = parts[1][:, LANES - 1 :]
    row = lax.broadcasted_iota(jnp.int32, (rows, LANES), 0)
    lane = lax.broadcasted_iota(jnp.int32, (rows, LANES), 1)
    place = lax.rem(row, 8) * STORE + mark.astype(jnp.int32) - 1
    pick = jnp.where((mark > 0.5) & (place == lane), 1.0, 0.0).astype(BF16)
    held[...] = lax.dot_general(
        pick,
        jnp.concatenate(parts, axis=1).astype(BF16),
        (((0,), (0,)), ((), ())),
        preferred_element_type=F32,
    )
    own = held[pl.ds(pl.multiple_of(mem_ref[0] * STORE, STORE), STORE)]
    logits = own[:, 2 * LANES : 3 * LANES] + own[:, 3 * LANES :]
    logits_ref[0] = logits[:, :LANGS]
    sim = lax.dot_general(
        own[:, :EMB].astype(BF16),
        held[: 8 * STORE, :EMB].astype(BF16),
        (((1,), (1,)), ((), ())),
        preferred_element_type=F32,
    )
    sim_ref[0] = sim / EMB


def home(member, recv):
    vmem = pl.BlockSpec(memory_space=pltpu.VMEM)
    return pl.pallas_call(
        home_kernel,
        out_shape=(
            jax.ShapeDtypeStruct((1, STORE, LANGS), F32),
            jax.ShapeDtypeStruct((1, STORE, 8 * STORE), F32),
        ),
        in_specs=[pl.BlockSpec(memory_space=pltpu.SMEM), vmem],
        out_specs=(vmem, vmem),
        scratch_shapes=[
            pltpu.VMEM(recv.shape, F32),
            pltpu.VMEM((LANES, 4 * LANES), F32),
        ],
        compiler_params=pltpu.CompilerParams(vmem_limit_bytes=16 << 20),
        name="home",
    )(member, recv)


def prepare(initial_conv_weight, branch_weight):
    tall = jnp.pad(initial_conv_weight, ((PAD_TOP, PAD_TOP), (0, 0)))
    early = jnp.pad(branch_weight, ((0, 0), (0, BR), (0, 0)))
    late = jnp.pad(branch_weight, ((0, 0), (BR, 0), (0, 0)))
    return tall, jnp.concatenate([early, late], axis=2)


def shards(
    filterbank,
    destination,
    initial_conv_weight,
    expand_weight,
    branch_weight,
    merge_weight,
    squeeze_weight,
    excite_weight,
    attend_weight,
    score_weight,
    embed_weight,
    language_weight,
):
    bank = filterbank.reshape(STORE, FLAT, LANES).transpose(1, 0, 2)
    bank = bank.reshape(FLAT * STORE, LANES)
    outbound = pack(bank, destination.reshape(STORE))
    arrived = lax.all_to_all(outbound, "grp", split_axis=0, concat_axis=0, tiled=True)
    tall, pairs = prepare(initial_conv_weight, branch_weight)
    scored = family(
        arrived,
        (
            tall,
            expand_weight,
            pairs,
            merge_weight,
            squeeze_weight,
            excite_weight,
            attend_weight[0],
            score_weight[0],
            embed_weight[0],
            language_weight[0],
        ),
    )
    back = lax.all_to_all(
        scored.reshape(SLOTS * 8, 4, LANES),
        ("grp", "mem"),
        split_axis=0,
        concat_axis=0,
        tiled=True,
    )
    member = lax.axis_index("mem").astype(jnp.int32).reshape(1)
    return home(member, back.reshape(SLOTS * 8 * 4, LANES))


def solution(mesh):
    return jax.shard_map(
        shards,
        mesh=mesh,
        in_specs=(
            P("grp", "mem", None, None),
            P("grp", "mem"),
            P(),
            P(),
            P(),
            P(),
            P(),
            P(),
            P("grp", None, None),
            P("grp", None, None),
            P("grp", None, None),
            P("grp", None, None),
        ),
        out_specs=(P("grp", "mem", None), P("grp", "mem", None)),
        check_vma=False,
    )
```
